256 devices in a mesh: dp: 4 (over z_hi), expert: 64 (over x, y, z_lo, core).
Axes of the slice: x: 4, y: 4, z: 8 (z_hi: 4, z_lo: 2; z = z_hi * 2 + z_lo), core: 2. Of those that a mesh axis runs over, the one named last changes fastest.
Arguments:
- tokens: bfloat16 [32768, 1536], P(('dp', 'expert')), may hold values from -6 to 6
- routes: int32 [32768, 2], P(('dp', 'expert')), may hold values from 0 to 63, all different within a row; in each aligned block of 128 rows (0 to 127, 128 to 255, ...) at most 5 rows name the same one
- combine: float32 [32768, 2], P(('dp', 'expert')), may hold values from 0.1 to 1
- w_gate: bfloat16 [64, 1536, 1536], P('expert', None, 'dp'), may hold values from -0.15625 to 0.15625
- w_up: bfloat16 [64, 1536, 1536], P('expert', None, 'dp'), may hold values from -0.15625 to 0.15625
- w_down: bfloat16 [64, 1536, 1536], P('expert', 'dp'), may hold values from -0.15625 to 0.15625
- cotangent: bfloat16 [32768, 1536], P(('dp', 'expert')), may hold values from -2 to 2
Outputs:
- out: bfloat16 [32768, 1536], P(('dp', 'expert'))
- d_tokens: bfloat16 [32768, 1536], P(('dp', 'expert'))
- d_combine: float32 [32768, 2], P(('dp', 'expert'))
- grad_gate: bfloat16 [64, 1536, 1536], P('expert', None, 'dp')
- grad_up: bfloat16 [64, 1536, 1536], P('expert', None, 'dp')
- grad_down: bfloat16 [64, 1536, 1536], P('expert', 'dp')
The draws below stay inside these ranges and needn't reach their ends.
Inputs may be any that keep to these rules, and one draw needn't show every extreme that they name: `routes`: the two experts of a token differ. Among the 128 tokens of one source block no expert is named more than 5 times, and in every draw some expert is named exactly 5 times by some source block.
All inputs are finite; a program needn't handle non-finite values.
Results may differ from the reference program's by a relative error of at most 0.013.
Values may be sent and summed in bfloat16 or wider, within the bound.
No kernel may reach another device: no remote copies, remote signals or barrier semaphores. Data moves between devices by JAX's collectives and lax.ppermute only.
A program may use at most 128 MiB of HBM per device.

```python
import math
import jax
import jax.numpy as jnp
import numpy as np
from jax import lax

D = 1536
FF = 1536
TOK_DEV = 128
EXPERTS = 64
CAP = 5
TOKENS = 32768
N_DP = 4
N_EXPERT = 64


def shard_levels(rng, extent, split, low, largest):
    gain, own = 1.0, jax.random.fold_in(rng, 6)
    for dim, blocks in split:
        steps = jnp.exp(jax.random.uniform(jax.random.fold_in(own, dim), (blocks,), jnp.float32, low / len(split), largest / len(split)))
        gain = gain * jnp.repeat(steps, extent[dim] // blocks).reshape([-1 if axis == dim else 1 for axis in range(len(extent))])
    return gain


def assign_block(key, own, number, rows, count, top, reach, lean):
    sequence = jax.random.permutation(key, count)
    heavy_load, usual = portions_of(count, rows * top, reach, lean, True), portions_of(count, rows * top, reach, lean, False)
    places = jnp.arange(count)

    def named(sizes, turn):
        used = int((sizes > 0).sum())
        fixed = max(1, used // 4)
        moved = fixed + (places - fixed + turn * (used - fixed)) % max(1, count - fixed)
        return jnp.zeros((count,), jnp.int32).at[sequence[jnp.where(places < fixed, places, moved)]].set(jnp.asarray(sizes, jnp.int32))

    sizes = jnp.where(number % 4 == 0, named(heavy_load, number // 4), named(usual, number - number // 4 - 1))
    mixed = jax.random.permutation(jax.random.fold_in(own, 3), count)
    giver, receiver = mixed[0:count // 2 * 2:2], mixed[1:count // 2 * 2:2]
    margin = jnp.minimum(sizes[giver] - 1, reach - sizes[receiver]) // 2
    margin = jnp.where((giver == sequence[0]) | (receiver == sequence[0]) | (sizes[receiver] == 0), 0, jnp.maximum(margin, 0))
    moved = jax.random.randint(jax.random.fold_in(own, 4), (count // 2,), 0, 1 << 20) % (margin + 1)
    sizes = sizes.at[giver].add(-moved).at[receiver].add(moved)
    labels = jnp.searchsorted(jnp.cumsum(sizes), jnp.arange(rows * top), side="right").astype(jnp.int32)
    table = labels.reshape(top, rows).T
    table = table[jax.random.permutation(jax.random.fold_in(own, 1), rows)]
    turn = jax.random.randint(jax.random.fold_in(own, 2), (rows, 1), 0, top)
    return jnp.take_along_axis(table, (jnp.arange(top)[None, :] + turn) % top, axis=1)


def portions_of(number_of, total, most, skew, full):
    weights = [(1 << 20) // math.isqrt(rank ** skew) + 1 for rank in range(1, number_of + 1)]
    largest = most if full else min(most, max(-(-total // number_of), total * weights[0] // sum(weights)))
    least = 1 if total - largest >= number_of - 1 else 0
    counts, rest = [largest] + [least] * (number_of - 1), total - largest - least * (number_of - 1)
    while rest > 0:
        candidates = [i for i in range(1, number_of) if counts[i] < largest] or [i for i in range(1, number_of) if counts[i] < most]
        mass, remaining = sum([weights[i] for i in candidates]), rest
        for i in candidates:
            addition = min(most - counts[i], max(1, remaining * weights[i] // mass), rest)
            counts[i] = counts[i] + addition
            rest = rest - addition
    return np.array(counts)


def gaussian(rng, shape, spread, most, pieces=(), held_as=jnp.bfloat16):
    values = spread * jax.random.normal(rng, shape, jnp.float32)
    if pieces:
        values = values * shard_levels(rng, shape, pieces, -0.22, 0.18)
    return jnp.clip(values, -most, most).astype(held_as)


def setup_inputs(seed: int = 0) -> dict:
    key_of = jax.random.split(jax.random.key(seed), 8)
    tokens = gaussian(key_of[0], (TOKENS, D), 1.0, 6.0, ((0, 256),))
    routes_keys = jax.random.split(jax.random.fold_in(key_of[1], 1), TOKENS // TOK_DEV)
    routes_turns = jax.random.permutation(jax.random.fold_in(key_of[1], 3), TOKENS // TOK_DEV)
    routes = jax.vmap(lambda own, number: assign_block(jax.random.fold_in(key_of[1], 2), own, number, TOK_DEV, EXPERTS, 2, CAP, 1))(routes_keys, routes_turns).reshape((TOKENS, 2))
    combine = jnp.clip(0.1 + 0.9 * jax.random.uniform(key_of[2], (TOKENS, 2), jnp.float32) ** shard_levels(key_of[2], (TOKENS, 2), ((0, 256),), -0.2, 0.2), 0.1, 1.0)
    w_gate = gaussian(key_of[3], (EXPERTS, D, FF), D ** -0.5, 0.15625, ((0, 64), (2, 4)))
    w_up = gaussian(key_of[4], (EXPERTS, D, FF), D ** -0.5, 0.15625, ((0, 64), (2, 4)))
    w_down = gaussian(key_of[5], (EXPERTS, FF, D), FF ** -0.5, 0.15625, ((0, 64), (1, 4)))
    cotangent = gaussian(key_of[6], (TOKENS, D), 0.3, 2.0, ((0, 256),))
    return {"tokens": tokens, "routes": routes, "combine": combine, "w_gate": w_gate, "w_up": w_up, "w_down": w_down, "cotangent": cotangent}


def block_slots(block_routes):
    ids = jnp.arange(EXPERTS, dtype=jnp.int32)
    onehot = (block_routes[:, None] == ids[None, :]).astype(jnp.int32)
    before = jnp.cumsum(onehot, axis=0) - onehot
    return jnp.sum(before * onehot, axis=1).astype(jnp.int32)


def group_total(left, right):
    left_groups = left.astype(jnp.float32).reshape(N_DP, -1, left.shape[1])
    right_groups = right.astype(jnp.float32).reshape(N_DP, -1, right.shape[1])
    part = jnp.einsum("gri,grj->gij", left_groups, right_groups)
    part = lax.optimization_barrier(part.astype(jnp.bfloat16)).astype(jnp.float32)
    return jnp.sum(part, axis=0).astype(jnp.bfloat16)


def reference(tokens, routes, combine, w_gate, w_up, w_down, cotangent):
    pair_count = 2 * TOKENS
    slots = lax.map(block_slots, routes.reshape(N_DP * N_EXPERT, 2 * TOK_DEV)).reshape(-1)
    flat = routes.reshape(-1).astype(jnp.int32)
    pairs = jnp.arange(pair_count, dtype=jnp.int32)
    target_row = (pairs // (2 * TOK_DEV)) * CAP + slots
    table = jnp.full((EXPERTS, N_DP * N_EXPERT * CAP), pair_count, jnp.int32)
    table = table.at[flat, target_row].set(pairs)
    combine_flat = combine.reshape(-1)

    def expert_step(carry, inputs):
        out_acc, back_acc, comb_acc = carry
        table_row, gate_w, up_w, down_w = inputs
        valid = table_row < pair_count
        safe = jnp.minimum(table_row, pair_count - 1).astype(jnp.int32)
        token_index = (safe // 2).astype(jnp.int32)
        weight = jnp.where(valid, combine_flat[safe], jnp.zeros((), combine_flat.dtype))
        token_rows = jnp.where(valid[:, None], tokens[token_index], jnp.zeros((), tokens.dtype))
        cot = cotangent[token_index].astype(jnp.float32)
        gate_pre = jnp.dot(token_rows, gate_w, preferred_element_type=jnp.float32)
        up_pre = jnp.dot(token_rows, up_w, preferred_element_type=jnp.float32)
        sigmoid_gate = jax.nn.sigmoid(gate_pre)
        hidden = (gate_pre * sigmoid_gate * up_pre).astype(jnp.bfloat16)
        expert_out = jnp.dot(hidden, down_w, preferred_element_type=jnp.float32).astype(jnp.bfloat16)
        result = expert_out.astype(jnp.float32)
        landing = jnp.where(valid, token_index, TOKENS).astype(jnp.int32)
        out_acc = out_acc.at[landing].add(weight[:, None] * result, mode="drop")
        dot_terms = jnp.sum(cot * result, axis=1)
        comb_acc = comb_acc.at[jnp.where(valid, table_row, pair_count).astype(jnp.int32)].set(dot_terms, mode="drop")
        cot_rows = (weight[:, None] * cot).astype(jnp.bfloat16)
        d_hidden = jnp.dot(cot_rows, down_w.T, preferred_element_type=jnp.float32)
        d_gate = (d_hidden * up_pre * sigmoid_gate * (1.0 + gate_pre * (1.0 - sigmoid_gate))).astype(jnp.bfloat16)
        d_up = (d_hidden * gate_pre * sigmoid_gate).astype(jnp.bfloat16)
        back_rows = (jnp.dot(d_gate, gate_w.T, preferred_element_type=jnp.float32)
                     + jnp.dot(d_up, up_w.T, preferred_element_type=jnp.float32)).astype(jnp.bfloat16)
        back_acc = back_acc.at[landing].add(back_rows.astype(jnp.float32), mode="drop")
        grads = (group_total(token_rows, d_gate), group_total(token_rows, d_up), group_total(hidden, cot_rows))
        return (out_acc, back_acc, comb_acc), grads

    start = (jnp.zeros((TOKENS, D), jnp.float32), jnp.zeros((TOKENS, D), jnp.float32),
             jnp.zeros((pair_count,), jnp.float32))
    final, grads = lax.scan(expert_step, start, (table, w_gate, w_up, w_down))
    out_acc, back_acc, comb_acc = final
    grad_gate, grad_up, grad_down = grads
    return (out_acc.astype(jnp.bfloat16), back_acc.astype(jnp.bfloat16), comb_acc.reshape(TOKENS, 2),
            grad_gate, grad_up, grad_down)
```

```python
import jax
import jax.numpy as jnp
from jax import lax
from jax.sharding import PartitionSpec as P


def dot_plain(left, right):
    return jnp.dot(left, right, preferred_element_type=jnp.float32)


def dot_last(left, right):
    return lax.dot_general(
        left, right, (((1,), (1,)), ((), ())), preferred_element_type=jnp.float32
    )


def dot_first(left, right):
    return lax.dot_general(
        left, right, (((0,), (0,)), ((), ())), preferred_element_type=jnp.float32
    )


def gate_grads(d_hidden, gate_pre, up_pre, sigmoid_gate):
    d_gate = (d_hidden * up_pre * sigmoid_gate * (1.0 + gate_pre * (1.0 - sigmoid_gate))).astype(
        jnp.bfloat16
    )
    d_up = (d_hidden * gate_pre * sigmoid_gate).astype(jnp.bfloat16)
    return (d_gate, d_up)


def column_of(expert):
    return expert // 4 * 2 + expert % 2


def pair_of(expert):
    return expert // 2 % 2


def on_device(tokens, routes, combine, w_gate, w_up, w_down, cotangent):
    experts = lax.axis_size("expert")
    groups = lax.axis_size("dp")
    count = tokens.shape[0]
    width = tokens.shape[1]
    capacity = 10 * count // (4 * experts)
    slot_total = experts * capacity
    row_total = groups * slot_total
    columns = experts // 2
    planes = 2 * groups
    column_groups = [
        [e for e in range(experts) if pair_of(e) == pair] for pair in range(2)
    ]
    ring_groups = [
        [g * experts + column // 2 * 4 + pair * 2 + column % 2 for g in range(groups) for pair in range(2)]
        for column in range(columns)
    ]
    everyone = ("dp", "expert")

    flat = routes.reshape(-1)
    onehot = (flat[:, None] == jnp.arange(experts, dtype=jnp.int32)[None, :]).astype(jnp.int32)
    before = jnp.cumsum(onehot, axis=0) - onehot
    slots = jnp.sum(before * onehot, axis=1).reshape(count, 2)
    target_row = routes * capacity + slots
    positions = jnp.arange(slot_total, dtype=jnp.int32)[:, None]
    pick_first = (positions == target_row[None, :, 0]).astype(jnp.bfloat16)
    pick_second = (positions == target_row[None, :, 1]).astype(jnp.bfloat16)

    info = jnp.concatenate([routes.T, slots.T], axis=0).astype(jnp.bfloat16)
    info = jnp.pad(info, ((0, 4), (0, width - count)))
    ring = lax.all_gather(
        jnp.concatenate([tokens, info], axis=0), everyone, axis_index_groups=ring_groups, axis=0, tiled=True
    )

    cot = cotangent.astype(jnp.float32)
    first_cot = (combine[:, 0:1] * cot).astype(jnp.bfloat16)
    second_cot = (combine[:, 1:2] * cot).astype(jnp.bfloat16)
    send_cot = (dot_plain(pick_first, first_cot) + dot_plain(pick_second, second_cot)).astype(
        jnp.bfloat16
    )
    got_cot = lax.all_to_all(
        send_cot.reshape(experts, capacity, width), "expert", split_axis=0, concat_axis=0, tiled=True
    ).reshape(slot_total, width)
    cot_rows = lax.all_gather(got_cot, "dp", axis=0, tiled=True)

    rows_held = count + 8
    held = ring.reshape(planes, rows_held, width)[:, count : count + 4, :count].astype(jnp.int32)
    block = jnp.arange(planes, dtype=jnp.int32)[:, None, None]
    ring_expert, ring_slot = held[:, 0:2], held[:, 2:4]
    ring_row = column_of(ring_expert) * (planes * capacity) + block * capacity + ring_slot
    here = pair_of(ring_expert) == pair_of(lax.axis_index("expert"))
    ring_row = jnp.where(here, ring_row, -1)
    held_row = jnp.pad(ring_row, ((0, 0), (0, 0), (0, 8)), constant_values=-1)
    row_ids = jnp.arange(row_total, dtype=jnp.int32)[:, None]
    held_row = held_row.transpose(1, 0, 2).reshape(2, 1, planes * rows_held)
    select = ((row_ids == held_row[0]) | (row_ids == held_row[1])).astype(jnp.bfloat16)
    send_tokens = dot_plain(select, ring).astype(jnp.bfloat16)
    token_rows = lax.all_to_all(
        send_tokens.reshape(columns, planes * capacity, width),
        "expert",
        split_axis=0,
        concat_axis=0,
        tiled=True,
        axis_index_groups=column_groups,
    ).reshape(row_total, width)

    ids = jnp.arange(row_total, dtype=jnp.int32)
    column, plane, slot = ids // (planes * capacity), ids // capacity % planes, ids % capacity
    source = column // 2 * 4 + plane % 2 * 2 + column % 2
    cot_place = (plane // 2 * experts + source) * capacity + slot
    to_token_order = (cot_place[:, None] == ids[None, :]).astype(jnp.bfloat16)

    gate_w, up_w, down_w = w_gate[0], w_up[0], w_down[0]
    gate_pre = dot_plain(token_rows, gate_w)
    up_pre = dot_plain(token_rows, up_w)
    sigmoid_gate = jax.nn.sigmoid(gate_pre)
    hidden = (gate_pre * sigmoid_gate * up_pre).astype(jnp.bfloat16)
    hidden_cot = dot_first(to_token_order, hidden).astype(jnp.bfloat16)
    part_out = dot_plain(hidden_cot, down_w).astype(jnp.bfloat16)
    expert_out = lax.psum_scatter(part_out, "dp", scatter_dimension=0, tiled=True)

    d_hidden = dot_last(cot_rows, down_w).astype(jnp.bfloat16)
    d_hidden = dot_plain(to_token_order, d_hidden)
    d_gate, d_up = gate_grads(d_hidden, gate_pre, up_pre, sigmoid_gate)
    back_rows = (dot_last(d_gate, gate_w) + dot_last(d_up, up_w)).astype(jnp.bfloat16)
    arrived = lax.all_to_all(
        back_rows.reshape(columns, planes * capacity, width),
        "expert",
        split_axis=0,
        concat_axis=0,
        tiled=True,
        axis_index_groups=column_groups,
    ).reshape(row_total, width)
    token_row = ring_row.transpose(1, 0, 2).reshape(2, planes * count, 1)
    add_up = ((token_row[0] == ids[None, :]) | (token_row[1] == ids[None, :])).astype(jnp.bfloat16)
    d_ring = dot_plain(add_up, arrived).astype(jnp.bfloat16)
    d_tokens = lax.psum_scatter(
        d_ring, everyone, axis_index_groups=ring_groups, scatter_dimension=0, tiled=True
    )

    returned = lax.all_to_all(
        expert_out.reshape(experts, capacity, width), "expert", split_axis=0, concat_axis=0, tiled=True
    ).reshape(slot_total, width)
    first_out = dot_first(pick_first, returned)
    second_out = dot_first(pick_second, returned)
    out = (combine[:, 0:1] * first_out + combine[:, 1:2] * second_out).astype(jnp.bfloat16)
    d_combine = jnp.stack(
        [jnp.sum(cot * first_out, axis=1), jnp.sum(cot * second_out, axis=1)], axis=1
    )

    grad_gate = dot_first(token_rows, d_gate).astype(jnp.bfloat16)
    grad_up = dot_first(token_rows, d_up).astype(jnp.bfloat16)
    grad_down = dot_first(hidden_cot, cot_rows).astype(jnp.bfloat16)
    return (out, d_tokens, d_combine, grad_gate[None], grad_up[None], grad_down[None])


def solution(mesh):
    placed = (
        P(("dp", "expert"), None),
        P(("dp", "expert"), None),
        P(("dp", "expert"), None),
        P("expert", None, "dp"),
        P("expert", None, "dp"),
        P("expert", "dp", None),
        P(("dp", "expert"), None),
    )
    return jax.shard_map(
        on_device,
        mesh=mesh,
        in_specs=placed,
        out_specs=(
            P(("dp", "expert"), None),
            P(("dp", "expert"), None),
            P(("dp", "expert"), None),
            P("expert", None, "dp"),
            P("expert", None, "dp"),
            P("expert", "dp", None),
        ),
        check_vma=False,
    )
```

```python
import jax
import jax.numpy as jnp
from jax import lax
from jax.experimental import pallas as pl
from jax.experimental.pallas import tpu as pltpu
from jax.sharding import PartitionSpec as P


def dot_plain(left, right):
    return jnp.dot(left, right, preferred_element_type=jnp.float32)


def dot_last(left, right):
    return lax.dot_general(
        left, right, (((1,), (1,)), ((), ())), preferred_element_type=jnp.float32
    )


def dot_first(left, right):
    return lax.dot_general(
        left, right, (((0,), (0,)), ((), ())), preferred_element_type=jnp.float32
    )


ROWS = 256


def forward_kernel(x_ref, w_ref, pre_ref, hidden_ref):
    pre = dot_plain(x_ref[...], w_ref[...])
    pre_ref[...] = pre
    half = pre.shape[1] // 2
    gate_pre, up_pre = pre[:, :half], pre[:, half:]
    hidden_ref[...] = (gate_pre * jax.nn.sigmoid(gate_pre) * up_pre).astype(jnp.bfloat16)


def forward(rows, weights):
    total, width = rows.shape
    both = weights.shape[1]
    return pl.pallas_call(
        forward_kernel,
        grid=(total // ROWS,),
        in_specs=[
            pl.BlockSpec((ROWS, width), lambda i: (i, 0)),
            pl.BlockSpec((width, both), lambda i: (0, 0), pipeline_mode=pl.Buffered(1)),
        ],
        out_specs=[
            pl.BlockSpec((ROWS, both), lambda i: (i, 0)),
            pl.BlockSpec((ROWS, both // 2), lambda i: (i, 0)),
        ],
        out_shape=[
            jax.ShapeDtypeStruct((total, both), jnp.float32),
            jax.ShapeDtypeStruct((total, both // 2), jnp.bfloat16),
        ],
        compiler_params=pltpu.CompilerParams(vmem_limit_bytes=24 << 20),
        name="forward_rows",
    )(rows, weights)


def backward_kernel(place_ref, d_ref, pre_ref, w_ref, grads_ref, back_ref):
    total = d_ref.shape[0]
    places = jnp.broadcast_to(place_ref[...], (ROWS, total))
    select = jnp.where(places == lax.broadcasted_iota(jnp.int32, (ROWS, total), 1), 1.0, 0.0)
    d_hidden = dot_plain(select.astype(jnp.bfloat16), d_ref[...])
    half = d_hidden.shape[1]
    gate_pre, up_pre = pre_ref[:, :half], pre_ref[:, half:]
    sigmoid_gate = jax.nn.sigmoid(gate_pre)
    d_gate = d_hidden * up_pre * sigmoid_gate * (1.0 + gate_pre * (1.0 - sigmoid_gate))
    d_up = d_hidden * gate_pre * sigmoid_gate
    grads_ref[:, :half] = d_gate.astype(jnp.bfloat16)
    grads_ref[:, half:] = d_up.astype(jnp.bfloat16)
    back_ref[...] = dot_plain(grads_ref[...], w_ref[...]).astype(jnp.bfloat16)


def backward(places, d_hidden, pre, weights):
    total, both = pre.shape
    width = weights.shape[1]
    return pl.pallas_call(
        backward_kernel,
        grid=(total // ROWS,),
        in_specs=[
            pl.BlockSpec((ROWS, 1), lambda i: (i, 0)),
            pl.BlockSpec((total, both // 2), lambda i: (0, 0), pipeline_mode=pl.Buffered(1)),
            pl.BlockSpec((ROWS, both), lambda i: (i, 0)),
            pl.BlockSpec((both, width), lambda i: (0, 0), pipeline_mode=pl.Buffered(1)),
        ],
        out_specs=[
            pl.BlockSpec((ROWS, both), lambda i: (i, 0)),
            pl.BlockSpec((ROWS, width), lambda i: (i, 0)),
        ],
        out_shape=[
            jax.ShapeDtypeStruct((total, both), jnp.bfloat16),
            jax.ShapeDtypeStruct((total, width), jnp.bfloat16),
        ],
        compiler_params=pltpu.CompilerParams(vmem_limit_bytes=24 << 20),
        name="backward_rows",
    )(places, d_hidden, pre, weights)


PADDED = 8


def prepare_kernel(tokens_ref, routes_ref, combine_ref, cot_ref, own_ref, send_ref, chosen_ref):
    count = tokens_ref.shape[0]
    square = (count, count)
    row, col = lax.broadcasted_iota(jnp.int32, square, 0), lax.broadcasted_iota(jnp.int32, square, 1)
    chosen = routes_ref[...].astype(jnp.float32)
    down = [jnp.broadcast_to(chosen[:, k : k + 1], square) for k in range(2)]
    across = [expert.T for expert in down]
    slots = [
        jnp.sum(
            jnp.where((row < col) & ((down[0] == expert) | (down[1] == expert)), 1.0, 0.0),
            axis=0,
            keepdims=True,
        )
        for expert in across
    ]
    own_ref[:count, :] = tokens_ref[...]
    own_ref[count:, :] = jnp.zeros((own_ref.shape[0] - count, own_ref.shape[1]), jnp.bfloat16)
    lines = [across[0][:1], across[1][:1], slots[0], slots[1], jnp.zeros((12, count), jnp.float32)]
    own_ref[count:, :count] = jnp.concatenate(lines, axis=0).astype(jnp.bfloat16)
    cot = cot_ref[...].astype(jnp.float32)
    total = None
    for k in range(2):
        expert, slot = across[k][:1].astype(jnp.int32), slots[k].astype(jnp.int32)
        chosen_ref[k : k + 1, :] = expert
        chosen_ref[k + 2 : k + 3, :] = slot
        quarter, last = lax.shift_right_logical(expert, 2), lax.bitwise_and(expert, 1)
        pair = lax.bitwise_and(lax.shift_right_logical(expert, 1), 1)
        places = ((quarter * 2 + last) * 2 + pair) * PADDED + slot
        places = jnp.broadcast_to(places, (send_ref.shape[0], count))
        pick = jnp.where(lax.broadcasted_iota(jnp.int32, places.shape, 0) == places, 1.0, 0.0)
        weighted = (combine_ref[:, k : k + 1] * cot).astype(jnp.bfloat16)
        part = dot_plain(pick.astype(jnp.bfloat16), weighted)
        total = part if total is None else total + part
    send_ref[...] = total.astype(jnp.bfloat16)


def prepare(tokens, routes, combine, cotangent, experts):
    count, width = tokens.shape
    return pl.pallas_call(
        prepare_kernel,
        out_shape=[
            jax.ShapeDtypeStruct((count + 16, width), jnp.bfloat16),
            jax.ShapeDtypeStruct((experts * PADDED, width), jnp.bfloat16),
            jax.ShapeDtypeStruct((4, count), jnp.int32),
        ],
        compiler_params=pltpu.CompilerParams(vmem_limit_bytes=24 << 20),
        name="prepare_rows",
    )(tokens, routes, combine, cotangent)


def column_of(expert):
    return expert // 4 * 2 + expert % 2


def pair_of(expert):
    return expert // 2 % 2


def ring_shift(x, step):
    groups, experts = lax.axis_size("dp"), lax.axis_size("expert")
    pairs = []
    for group in range(groups):
        for expert in range(experts):
            z = (group * 2 + pair_of(expert) + step) % (2 * groups)
            target = z // 2 * experts + expert // 4 * 4 + z % 2 * 2 + expert % 2
            pairs.append((group * experts + expert, target))
    return lax.ppermute(x, ("dp", "expert"), pairs)


def group_shift(x, step):
    groups = lax.axis_size("dp")
    return lax.ppermute(x, "dp", [(g, (g + step) % groups) for g in range(groups)])


def pair_swap(x):
    experts = lax.axis_size("expert")
    return lax.ppermute(x, "expert", [(e, e + 2 - pair_of(e) * 4) for e in range(experts)])


def sum_of(*parts):
    total = parts[0].astype(jnp.float32)
    for part in parts[1:]:
        total = total + part.astype(jnp.float32)
    return total.astype(jnp.bfloat16)


def join(size, blocks):
    whole = jnp.zeros((size, blocks[0][1].shape[1]), blocks[0][1].dtype)
    for start, block in blocks:
        whole = lax.dynamic_update_slice_in_dim(whole, block, start, 0)
    return whole


def on_device(tokens, routes, combine, w_gate, w_up, w_down, cotangent):
    experts = lax.axis_size("expert")
    groups = lax.axis_size("dp")
    count = tokens.shape[0]
    width = tokens.shape[1]
    capacity = 10 * count // (4 * experts)
    slot_total = experts * capacity
    row_total = groups * slot_total
    columns = experts // 2
    planes = 2 * groups
    column_groups = [[e for e in range(experts) if pair_of(e) == pair] for pair in range(2)]
    ring_groups = [
        [g * experts + column // 2 * 4 + pair * 2 + column % 2 for g in range(groups) for pair in range(2)]
        for column in range(columns)
    ]
    everyone = ("dp", "expert")
    group = lax.axis_index("dp")
    place = lax.axis_index("expert")
    z = group * 2 + pair_of(place)

    own, send_cot, chosen = prepare(tokens, routes, combine, cotangent, experts)
    pair = pair_of(place)
    got = lax.all_to_all(
        send_cot.reshape(columns, 2 * PADDED, width),
        "expert",
        split_axis=0,
        concat_axis=0,
        tiled=True,
        axis_index_groups=column_groups,
    )
    got = [got[:, k * PADDED : k * PADDED + capacity].reshape(slot_total // 2, width) for k in range(2)]
    kept, passed = jnp.where(pair == 0, got[0], got[1]), jnp.where(pair == 0, got[1], got[0])
    got_cot = jnp.concatenate([kept, pair_swap(passed)], axis=0)
    cot = cotangent.astype(jnp.float32)
    target_row = (column_of(chosen[:2]) * 2 + (pair_of(chosen[:2]) != pair)) * capacity + chosen[2:]
    positions = jnp.arange(slot_total, dtype=jnp.int32)[:, None]
    pick_first = (positions == target_row[0:1]).astype(jnp.bfloat16)
    pick_second = (positions == target_row[1:2]).astype(jnp.bfloat16)

    held_count = count + 16
    ring = lax.all_gather(own, everyone, axis_index_groups=ring_groups, axis=0, tiled=True)

    half_rows = slot_total // 2
    cot_rows = lax.all_gather(got_cot, "dp", axis=0, tiled=True)

    held = ring.reshape(planes, held_count, width)[:, count : count + 4, :count].astype(jnp.int32)
    block = jnp.arange(planes, dtype=jnp.int32)[:, None, None]
    ring_expert, ring_slot = held[:, 0:2], held[:, 2:4]
    ring_row = column_of(ring_expert) * (planes * capacity) + block * capacity + ring_slot
    here = pair_of(ring_expert) == pair_of(place)
    ring_row = jnp.where(here, ring_row, -1)
    held_row = jnp.pad(ring_row, ((0, 0), (0, 0), (0, held_count - count)), constant_values=-1)
    held_row = held_row.transpose(1, 0, 2).reshape(2, 1, planes * held_count)
    row_ids = jnp.arange(row_total, dtype=jnp.int32)[:, None]
    select = ((row_ids == held_row[0]) | (row_ids == held_row[1])).astype(jnp.bfloat16)
    send_tokens = dot_plain(select, ring).astype(jnp.bfloat16)
    token_rows = lax.all_to_all(
        send_tokens.reshape(columns, planes * capacity, width),
        "expert",
        split_axis=0,
        concat_axis=0,
        tiled=True,
        axis_index_groups=column_groups,
    ).reshape(row_total, width)

    ids = jnp.arange(row_total, dtype=jnp.int32)
    column, plane, slot = ids // (planes * capacity), ids // capacity % planes, ids % capacity
    cot_place = (plane // 2 * 2 + (plane % 2 != pair)) * (slot_total // 2) + column * capacity + slot
    to_token_order = (cot_place[:, None] == ids[None, :]).astype(jnp.bfloat16)

    down_w = w_down[0]
    up_gate_w = jnp.concatenate([w_gate[0], w_up[0]], axis=1)
    up_gate_wt = jnp.concatenate([w_gate[0].T, w_up[0].T], axis=0)
    pre, hidden = forward(token_rows, up_gate_w)
    hidden_cot = dot_first(to_token_order, hidden).astype(jnp.bfloat16)
    part_out = dot_plain(hidden_cot, down_w).astype(jnp.bfloat16)
    expert_out = lax.psum_scatter(part_out, "dp", scatter_dimension=0, tiled=True)

    d_hidden = dot_last(cot_rows, down_w).astype(jnp.bfloat16)
    d_hidden, _ = lax.optimization_barrier((d_hidden, part_out))
    d_both, back_rows = backward(cot_place[:, None], d_hidden, pre, up_gate_wt)
    d_gate, d_up = d_both[:, : down_w.shape[0]], d_both[:, down_w.shape[0] :]
    arrived = lax.all_to_all(
        back_rows.reshape(columns, planes * capacity, width),
        "expert",
        split_axis=0,
        concat_axis=0,
        tiled=True,
        axis_index_groups=column_groups,
    ).reshape(row_total, width)
    token_row = ring_row.transpose(1, 0, 2).reshape(2, planes * count, 1)
    add_up = ((token_row[0] == ids[None, :]) | (token_row[1] == ids[None, :])).astype(jnp.bfloat16)
    d_ring = dot_plain(add_up, arrived).astype(jnp.bfloat16)
    d_tokens = lax.psum_scatter(
        d_ring, everyone, axis_index_groups=ring_groups, scatter_dimension=0, tiled=True
    )

    half_rows = slot_total // 2
    from_pair = [expert_out[:half_rows], pair_swap(expert_out[half_rows:])]
    from_pair = [rows.reshape(columns, 1, capacity, width) for rows in from_pair]
    returned = lax.all_to_all(
        jnp.concatenate(from_pair, axis=1).reshape(columns, 2 * capacity, width),
        "expert",
        split_axis=0,
        concat_axis=0,
        tiled=True,
        axis_index_groups=column_groups,
    ).reshape(slot_total, width)
    first_out = dot_first(pick_first, returned)
    second_out = dot_first(pick_second, returned)
    out = (combine[:, 0:1] * first_out + combine[:, 1:2] * second_out).astype(jnp.bfloat16)
    d_combine = jnp.stack(
        [jnp.sum(cot * first_out, axis=1), jnp.sum(cot * second_out, axis=1)], axis=1
    )

    grad_gate = dot_first(token_rows, d_gate).astype(jnp.bfloat16)
    grad_up = dot_first(token_rows, d_up).astype(jnp.bfloat16)
    grad_down = dot_first(hidden_cot, cot_rows).astype(jnp.bfloat16)
    return (out, d_tokens, d_combine, grad_gate[None], grad_up[None], grad_down[None])


def solution(mesh):
    placed = (
        P(("dp", "expert"), None),
        P(("dp", "expert"), None),
        P(("dp", "expert"), None),
        P("expert", None, "dp"),
        P("expert", None, "dp"),
        P("expert", "dp", None),
        P(("dp", "expert"), None),
    )
    return jax.shard_map(
        on_device,
        mesh=mesh,
        in_specs=placed,
        out_specs=(
            P(("dp", "expert"), None),
            P(("dp", "expert"), None),
            P(("dp", "expert"), None),
            P("expert", None, "dp"),
            P("expert", None, "dp"),
            P("expert", "dp", None),
        ),
        check_vma=False,
    )
```

```python
import jax
import jax.numpy as jnp
from jax import lax
from jax.experimental import pallas as pl
from jax.experimental.pallas import tpu as pltpu
from jax.sharding import PartitionSpec as P


def dot_plain(left, right):
    return jnp.dot(left, right, preferred_element_type=jnp.float32)


def dot_last(left, right):
    return lax.dot_general(
        left, right, (((1,), (1,)), ((), ())), preferred_element_type=jnp.float32
    )


def dot_first(left, right):
    return lax.dot_general(
        left, right, (((0,), (0,)), ((), ())), preferred_element_type=jnp.float32
    )


ROWS = 256


def forward_kernel(x_ref, w_ref, pre_ref, hidden_ref):
    pre = dot_plain(x_ref[...], w_ref[...])
    pre_ref[...] = pre
    half = pre.shape[1] // 2
    gate_pre, up_pre = pre[:, :half], pre[:, half:]
    hidden_ref[...] = (gate_pre * jax.nn.sigmoid(gate_pre) * up_pre).astype(jnp.bfloat16)


def forward(rows, weights):
    total, width = rows.shape
    both = weights.shape[1]
    return pl.pallas_call(
        forward_kernel,
        grid=(total // ROWS,),
        in_specs=[
            pl.BlockSpec((ROWS, width), lambda i: (i, 0)),
            pl.BlockSpec((width, both), lambda i: (0, 0), pipeline_mode=pl.Buffered(1)),
        ],
        out_specs=[
            pl.BlockSpec((ROWS, both), lambda i: (i, 0)),
            pl.BlockSpec((ROWS, both // 2), lambda i: (i, 0)),
        ],
        out_shape=[
            jax.ShapeDtypeStruct((total, both), jnp.float32),
            jax.ShapeDtypeStruct((total, both // 2), jnp.bfloat16),
        ],
        compiler_params=pltpu.CompilerParams(vmem_limit_bytes=24 << 20),
        name="forward_rows",
    )(rows, weights)


def backward_kernel(place_ref, d_ref, pre_ref, w_ref, grads_ref, back_ref):
    total = d_ref.shape[0]
    places = jnp.broadcast_to(place_ref[...], (ROWS, total))
    select = jnp.where(places == lax.broadcasted_iota(jnp.int32, (ROWS, total), 1), 1.0, 0.0)
    d_hidden = dot_plain(select.astype(jnp.bfloat16), d_ref[...])
    half = d_hidden.shape[1]
    gate_pre, up_pre = pre_ref[:, :half], pre_ref[:, half:]
    sigmoid_gate = jax.nn.sigmoid(gate_pre)
    d_gate = d_hidden * up_pre * sigmoid_gate * (1.0 + gate_pre * (1.0 - sigmoid_gate))
    d_up = d_hidden * gate_pre * sigmoid_gate
    grads_ref[:, :half] = d_gate.astype(jnp.bfloat16)
    grads_ref[:, half:] = d_up.astype(jnp.bfloat16)
    back_ref[...] = dot_plain(grads_ref[...], w_ref[...]).astype(jnp.bfloat16)


def backward(places, d_hidden, pre, weights):
    total, both = pre.shape
    width = weights.shape[1]
    return pl.pallas_call(
        backward_kernel,
        grid=(total // ROWS,),
        in_specs=[
            pl.BlockSpec((ROWS, 1), lambda i: (i, 0)),
            pl.BlockSpec((total, both // 2), lambda i: (0, 0), pipeline_mode=pl.Buffered(1)),
            pl.BlockSpec((ROWS, both), lambda i: (i, 0)),
            pl.BlockSpec((both, width), lambda i: (0, 0), pipeline_mode=pl.Buffered(1)),
        ],
        out_specs=[
            pl.BlockSpec((ROWS, both), lambda i: (i, 0)),
            pl.BlockSpec((ROWS, width), lambda i: (i, 0)),
        ],
        out_shape=[
            jax.ShapeDtypeStruct((total, both), jnp.bfloat16),
            jax.ShapeDtypeStruct((total, width), jnp.bfloat16),
        ],
        compiler_params=pltpu.CompilerParams(vmem_limit_bytes=24 << 20),
        name="backward_rows",
    )(places, d_hidden, pre, weights)


def outward_kernel(place_ref, hidden_ref, w_ref, out_ref):
    total = hidden_ref.shape[0]
    places = jnp.broadcast_to(place_ref[...], (ROWS, total))
    select = jnp.where(places == lax.broadcasted_iota(jnp.int32, (ROWS, total), 1), 1.0, 0.0)
    hidden = dot_plain(select.astype(jnp.bfloat16), hidden_ref[...]).astype(jnp.bfloat16)
    out_ref[...] = dot_plain(hidden, w_ref[...]).astype(jnp.bfloat16)


def outward(places, hidden, weights):
    total, part = hidden.shape
    width = weights.shape[1]
    return pl.pallas_call(
        outward_kernel,
        grid=(total // ROWS,),
        in_specs=[
            pl.BlockSpec((ROWS, 1), lambda i: (i, 0)),
            pl.BlockSpec((total, part), lambda i: (0, 0), pipeline_mode=pl.Buffered(1)),
            pl.BlockSpec((part, width), lambda i: (0, 0), pipeline_mode=pl.Buffered(1)),
        ],
        out_specs=pl.BlockSpec((ROWS, width), lambda i: (i, 0)),
        out_shape=jax.ShapeDtypeStruct((total, width), jnp.bfloat16),
        compiler_params=pltpu.CompilerParams(vmem_limit_bytes=24 << 20),
        name="outward_rows",
    )(places, hidden, weights)


PADDED = 8


def prepare_kernel(tokens_ref, routes_ref, combine_ref, cot_ref, own_ref, send_ref, chosen_ref):
    count = tokens_ref.shape[0]
    square = (count, count)
    row, col = lax.broadcasted_iota(jnp.int32, square, 0), lax.broadcasted_iota(jnp.int32, square, 1)
    chosen = routes_ref[...].astype(jnp.float32)
    down = [jnp.broadcast_to(chosen[:, k : k + 1], square) for k in range(2)]
    across = [expert.T for expert in down]
    slots = [
        jnp.sum(
            jnp.where((row < col) & ((down[0] == expert) | (down[1] == expert)), 1.0, 0.0),
            axis=0,
            keepdims=True,
        )
        for expert in across
    ]
    own_ref[:count, :] = tokens_ref[...]
    own_ref[count:, :] = jnp.zeros((own_ref.shape[0] - count, own_ref.shape[1]), jnp.bfloat16)
    lines = [across[0][:1], across[1][:1], slots[0], slots[1], jnp.zeros((12, count), jnp.float32)]
    own_ref[count:, :count] = jnp.concatenate(lines, axis=0).astype(jnp.bfloat16)
    cot = cot_ref[...].astype(jnp.float32)
    total = None
    for k in range(2):
        expert, slot = across[k][:1].astype(jnp.int32), slots[k].astype(jnp.int32)
        chosen_ref[k : k + 1, :] = expert
        chosen_ref[k + 2 : k + 3, :] = slot
        quarter, last = lax.shift_right_logical(expert, 2), lax.bitwise_and(expert, 1)
        pair = lax.bitwise_and(lax.shift_right_logical(expert, 1), 1)
        places = ((quarter * 2 + last) * 2 + pair) * PADDED + slot
        places = jnp.broadcast_to(places, (send_ref.shape[0], count))
        pick = jnp.where(lax.broadcasted_iota(jnp.int32, places.shape, 0) == places, 1.0, 0.0)
        weighted = (combine_ref[:, k : k + 1] * cot).astype(jnp.bfloat16)
        part = dot_plain(pick.astype(jnp.bfloat16), weighted)
        total = part if total is None else total + part
    send_ref[...] = total.astype(jnp.bfloat16)


def prepare(tokens, routes, combine, cotangent, experts):
    count, width = tokens.shape
    return pl.pallas_call(
        prepare_kernel,
        out_shape=[
            jax.ShapeDtypeStruct((count + 16, width), jnp.bfloat16),
            jax.ShapeDtypeStruct((experts * PADDED, width), jnp.bfloat16),
            jax.ShapeDtypeStruct((4, count), jnp.int32),
        ],
        compiler_params=pltpu.CompilerParams(vmem_limit_bytes=24 << 20),
        name="prepare_rows",
    )(tokens, routes, combine, cotangent)


def column_of(expert):
    return expert // 4 * 2 + expert % 2


def pair_of(expert):
    return expert // 2 % 2


def ring_shift(x, step):
    groups, experts = lax.axis_size("dp"), lax.axis_size("expert")
    pairs = []
    for group in range(groups):
        for expert in range(experts):
            z = (group * 2 + pair_of(expert) + step) % (2 * groups)
            target = z // 2 * experts + expert // 4 * 4 + z % 2 * 2 + expert % 2
            pairs.append((group * experts + expert, target))
    return lax.ppermute(x, ("dp", "expert"), pairs)


def group_shift(x, step):
    groups = lax.axis_size("dp")
    return lax.ppermute(x, "dp", [(g, (g + step) % groups) for g in range(groups)])


def pair_swap(x):
    experts = lax.axis_size("expert")
    return lax.ppermute(x, "expert", [(e, e + 2 - pair_of(e) * 4) for e in range(experts)])


def sum_of(*parts):
    total = parts[0].astype(jnp.float32)
    for part in parts[1:]:
        total = total + part.astype(jnp.float32)
    return total.astype(jnp.bfloat16)


def join(size, blocks):
    whole = jnp.zeros((size, blocks[0][1].shape[1]), blocks[0][1].dtype)
    for start, block in blocks:
        whole = lax.dynamic_update_slice_in_dim(whole, block, start, 0)
    return whole


def on_device(tokens, routes, combine, w_gate, w_up, w_down, cotangent):
    experts = lax.axis_size("expert")
    groups = lax.axis_size("dp")
    count = tokens.shape[0]
    width = tokens.shape[1]
    capacity = 10 * count // (4 * experts)
    slot_total = experts * capacity
    row_total = groups * slot_total
    columns = experts // 2
    planes = 2 * groups
    column_groups = [[e for e in range(experts) if pair_of(e) == pair] for pair in range(2)]
    ring_groups = [
        [g * experts + column // 2 * 4 + pair * 2 + column % 2 for g in range(groups) for pair in range(2)]
        for column in range(columns)
    ]
    everyone = ("dp", "expert")
    group = lax.axis_index("dp")
    place = lax.axis_index("expert")
    z = group * 2 + pair_of(place)

    own, send_cot, chosen = prepare(tokens, routes, combine, cotangent, experts)
    pair = pair_of(place)
    got = lax.all_to_all(
        send_cot.reshape(columns, 2 * PADDED, width),
        "expert",
        split_axis=0,
        concat_axis=0,
        tiled=True,
        axis_index_groups=column_groups,
    )
    got = [got[:, k * PADDED : k * PADDED + capacity].reshape(slot_total // 2, width) for k in range(2)]
    kept, passed = jnp.where(pair == 0, got[0], got[1]), jnp.where(pair == 0, got[1], got[0])
    cot = cotangent.astype(jnp.float32)
    target_row = (column_of(chosen[:2]) * 2 + (pair_of(chosen[:2]) != pair)) * capacity + chosen[2:]
    positions = jnp.arange(slot_total, dtype=jnp.int32)[:, None]
    pick_first = (positions == target_row[0:1]).astype(jnp.bfloat16)
    pick_second = (positions == target_row[1:2]).astype(jnp.bfloat16)

    held_count = count + 16
    ring = lax.all_gather(own, everyone, axis_index_groups=ring_groups, axis=0, tiled=True)

    half_rows = slot_total // 2
    far_rows = half_rows // 2
    ring, kept, passed = lax.optimization_barrier((ring, kept, passed))
    passed = pair_swap(passed)
    cot_ahead, cot_behind = group_shift(kept, 1), group_shift(kept, -1)
    cot_far_a = group_shift(cot_ahead[:far_rows], 1)
    cot_far_b = group_shift(cot_behind[far_rows:], -1)
    far = (group + 2) % groups * half_rows
    cot_rows = join(
        row_total // 2,
        [
            (group * half_rows, kept),
            ((group - 1) % groups * half_rows, cot_ahead),
            ((group + 1) % groups * half_rows, cot_behind),
            (far, cot_far_a),
            (far + far_rows, cot_far_b),
        ],
    )

    held = ring.reshape(planes, held_count, width)[:, count : count + 4, :count].astype(jnp.int32)
    block = jnp.arange(planes, dtype=jnp.int32)[:, None, None]
    ring_expert, ring_slot = held[:, 0:2], held[:, 2:4]
    ring_row = column_of(ring_expert) * (planes * capacity) + block * capacity + ring_slot
    here = pair_of(ring_expert) == pair_of(place)
    ring_row = jnp.where(here, ring_row, -1)
    held_row = jnp.pad(ring_row, ((0, 0), (0, 0), (0, held_count - count)), constant_values=-1)
    held_row = held_row.transpose(1, 0, 2).reshape(2, 1, planes * held_count)
    row_ids = jnp.arange(row_total, dtype=jnp.int32)[:, None]
    select = ((row_ids == held_row[0]) | (row_ids == held_row[1])).astype(jnp.bfloat16)
    send_tokens = dot_plain(select, ring).astype(jnp.bfloat16)
    send_tokens, passed = lax.optimization_barrier((send_tokens, passed))
    token_rows = lax.all_to_all(
        send_tokens.reshape(columns, planes * capacity, width),
        "expert",
        split_axis=0,
        concat_axis=0,
        tiled=True,
        axis_index_groups=column_groups,
    ).reshape(row_total, width)

    token_rows, cot_rows = lax.optimization_barrier((token_rows, cot_rows))
    cot_rows = (cot_rows, lax.all_gather(passed, "dp", axis=0, tiled=True))

    ids = jnp.arange(row_total, dtype=jnp.int32)
    column, plane, slot = ids // (planes * capacity), ids // capacity % planes, ids % capacity
    cot_place = ((plane % 2 != pair) * groups + plane // 2) * half_rows + column * capacity + slot
    side = ids // half_rows % 2
    out_plane = ids // slot_total * 2 + jnp.where(side == 1, 1 - pair, pair)
    out_place = (ids % half_rows // capacity * planes + out_plane) * capacity + ids % capacity

    down_w = w_down[0]
    up_gate_w = jnp.concatenate([w_gate[0], w_up[0]], axis=1)
    up_gate_wt = jnp.concatenate([w_gate[0].T, w_up[0].T], axis=0)
    pre, hidden = forward(token_rows, up_gate_w)
    part_out = outward(out_place[:, None], hidden, down_w)
    expert_out = lax.psum_scatter(part_out, "dp", scatter_dimension=0, tiled=True)

    d_hidden = jnp.concatenate([dot_last(rows, down_w).astype(jnp.bfloat16) for rows in cot_rows], axis=0)
    d_hidden, _ = lax.optimization_barrier((d_hidden, part_out))
    d_both, back_rows = backward(cot_place[:, None], d_hidden, pre, up_gate_wt)
    d_gate, d_up = d_both[:, : down_w.shape[0]], d_both[:, down_w.shape[0] :]
    arrived = lax.all_to_all(
        back_rows.reshape(columns, planes * capacity, width),
        "expert",
        split_axis=0,
        concat_axis=0,
        tiled=True,
        axis_index_groups=column_groups,
    ).reshape(row_total, width)
    token_row = ring_row.transpose(1, 0, 2).reshape(2, planes * count, 1)
    add_up = ((token_row[0] == ids[None, :]) | (token_row[1] == ids[None, :])).astype(jnp.bfloat16)
    d_ring = dot_plain(add_up, arrived).astype(jnp.bfloat16)
    d_tokens = lax.psum_scatter(
        d_ring, everyone, axis_index_groups=ring_groups, scatter_dimension=0, tiled=True
    )

    half_rows = slot_total // 2
    from_pair = [expert_out[:half_rows], pair_swap(expert_out[half_rows:])]
    from_pair = [rows.reshape(columns, 1, capacity, width) for rows in from_pair]
    returned = lax.all_to_all(
        jnp.concatenate(from_pair, axis=1).reshape(columns, 2 * capacity, width),
        "expert",
        split_axis=0,
        concat_axis=0,
        tiled=True,
        axis_index_groups=column_groups,
    ).reshape(slot_total, width)
    first_out = dot_first(pick_first, returned)
    second_out = dot_first(pick_second, returned)
    out = (combine[:, 0:1] * first_out + combine[:, 1:2] * second_out).astype(jnp.bfloat16)
    d_combine = jnp.stack(
        [jnp.sum(cot * first_out, axis=1), jnp.sum(cot * second_out, axis=1)], axis=1
    )

    grad_gate = dot_first(token_rows, d_gate).astype(jnp.bfloat16)
    grad_up = dot_first(token_rows, d_up).astype(jnp.bfloat16)
    to_token_order = (cot_place[:, None] == ids[None, :]).astype(jnp.bfloat16)
    hidden_cot = dot_first(to_token_order, hidden).astype(jnp.bfloat16)
    grad_down = (
        dot_first(hidden_cot[: row_total // 2], cot_rows[0]) + dot_first(hidden_cot[row_total // 2 :], cot_rows[1])
    ).astype(jnp.bfloat16)
    return (out, d_tokens, d_combine, grad_gate[None], grad_up[None], grad_down[None])


def solution(mesh):
    placed = (
        P(("dp", "expert"), None),
        P(("dp", "expert"), None),
        P(("dp", "expert"), None),
        P("expert", None, "dp"),
        P("expert", None, "dp"),
        P("expert", "dp", None),
        P(("dp", "expert"), None),
    )
    return jax.shard_map(
        on_device,
        mesh=mesh,
        in_specs=placed,
        out_specs=(
            P(("dp", "expert"), None),
            P(("dp", "expert"), None),
            P(("dp", "expert"), None),
            P("expert", None, "dp"),
            P("expert", None, "dp"),
            P("expert", "dp", None),
        ),
        check_vma=False,
    )
```

```python
import functools
import jax
import jax.numpy as jnp
from jax import lax
from jax.experimental import pallas as pl
from jax.experimental.pallas import tpu as pltpu
from jax.sharding import PartitionSpec as P


def dot_plain(left, right):
    return jnp.dot(left, right, preferred_element_type=jnp.float32)


def dot_last(left, right):
    return lax.dot_general(
        left, right, (((1,), (1,)), ((), ())), preferred_element_type=jnp.float32
    )


def dot_first(left, right):
    return lax.dot_general(
        left, right, (((0,), (0,)), ((), ())), preferred_element_type=jnp.float32
    )


ROWS = 256


def forward_kernel(x_ref, w_ref, pre_ref, hidden_ref):
    pre = dot_plain(x_ref[...], w_ref[...])
    pre_ref[...] = pre
    half = pre.shape[1] // 2
    gate_pre, up_pre = pre[:, :half], pre[:, half:]
    hidden_ref[...] = (gate_pre * jax.nn.sigmoid(gate_pre) * up_pre).astype(jnp.bfloat16)


def forward(rows, weights):
    total, width = rows.shape
    both = weights.shape[1]
    return pl.pallas_call(
        forward_kernel,
        grid=(total // ROWS,),
        in_specs=[
            pl.BlockSpec((ROWS, width), lambda i: (i, 0)),
            pl.BlockSpec((width, both), lambda i: (0, 0), pipeline_mode=pl.Buffered(1)),
        ],
        out_specs=[
            pl.BlockSpec((ROWS, both), lambda i: (i, 0)),
            pl.BlockSpec((ROWS, both // 2), lambda i: (i, 0)),
        ],
        out_shape=[
            pltpu.HBM((total, both), jnp.float32),
            jax.ShapeDtypeStruct((total, both // 2), jnp.bfloat16),
        ],
        compiler_params=pltpu.CompilerParams(vmem_limit_bytes=24 << 20),
        name="forward_rows",
    )(rows, weights)


def backward_kernel(place_ref, d_ref, pre_ref, w_ref, grads_ref, back_ref):
    total = d_ref.shape[0]
    places = jnp.broadcast_to(place_ref[...], (ROWS, total))
    select = jnp.where(places == lax.broadcasted_iota(jnp.int32, (ROWS, total), 1), 1.0, 0.0)
    d_hidden = dot_plain(select.astype(jnp.bfloat16), d_ref[...])
    half = d_hidden.shape[1]
    gate_pre, up_pre = pre_ref[:, :half], pre_ref[:, half:]
    sigmoid_gate = jax.nn.sigmoid(gate_pre)
    d_gate = d_hidden * up_pre * sigmoid_gate * (1.0 + gate_pre * (1.0 - sigmoid_gate))
    d_up = d_hidden * gate_pre * sigmoid_gate
    grads_ref[:, :half] = d_gate.astype(jnp.bfloat16)
    grads_ref[:, half:] = d_up.astype(jnp.bfloat16)
    back_ref[...] = dot_plain(grads_ref[...], w_ref[...]).astype(jnp.bfloat16)


def backward(places, d_hidden, pre, weights):
    total, both = pre.shape
    width = weights.shape[1]
    return pl.pallas_call(
        backward_kernel,
        grid=(total // ROWS,),
        in_specs=[
            pl.BlockSpec((ROWS, 1), lambda i: (i, 0)),
            pl.BlockSpec((total, both // 2), lambda i: (0, 0), pipeline_mode=pl.Buffered(1)),
            pl.BlockSpec((ROWS, both), lambda i: (i, 0)),
            pl.BlockSpec((both, width), lambda i: (0, 0), pipeline_mode=pl.Buffered(1)),
        ],
        out_specs=[
            pl.BlockSpec((ROWS, both), lambda i: (i, 0)),
            pl.BlockSpec((ROWS, width), lambda i: (i, 0)),
        ],
        out_shape=[
            pltpu.HBM((total, both), jnp.bfloat16),
            pltpu.HBM((total, width), jnp.bfloat16),
        ],
        compiler_params=pltpu.CompilerParams(vmem_limit_bytes=24 << 20),
        name="backward_rows",
    )(places, d_hidden, pre, weights)


def outward_kernel(place_ref, hidden_ref, w_ref, hidden_out_ref, out_ref):
    total = hidden_ref.shape[0]
    places = jnp.broadcast_to(place_ref[...], (ROWS, total))
    select = jnp.where(places == lax.broadcasted_iota(jnp.int32, (ROWS, total), 1), 1.0, 0.0)
    hidden = dot_plain(select.astype(jnp.bfloat16), hidden_ref[...]).astype(jnp.bfloat16)
    hidden_out_ref[...] = hidden
    out_ref[...] = dot_plain(hidden, w_ref[...]).astype(jnp.bfloat16)


def outward(places, hidden, weights):
    total, part = hidden.shape
    width = weights.shape[1]
    return pl.pallas_call(
        outward_kernel,
        grid=(total // ROWS,),
        in_specs=[
            pl.BlockSpec((ROWS, 1), lambda i: (i, 0)),
            pl.BlockSpec((total, part), lambda i: (0, 0), pipeline_mode=pl.Buffered(1)),
            pl.BlockSpec((part, width), lambda i: (0, 0), pipeline_mode=pl.Buffered(1)),
        ],
        out_specs=[
            pl.BlockSpec((ROWS, part), lambda i: (i, 0)),
            pl.BlockSpec((ROWS, width), lambda i: (i, 0)),
        ],
        out_shape=[
            jax.ShapeDtypeStruct((total, part), jnp.bfloat16),
            pltpu.HBM((total, width), jnp.bfloat16),
        ],
        compiler_params=pltpu.CompilerParams(vmem_limit_bytes=24 << 20),
        name="outward_rows",
    )(places, hidden, weights)


PADDED = 8
INFO = 8


def spread_kernel(capacity, mine_ref, other_ref, out_ref):
    half, total = other_ref.shape[0], out_ref.shape[0]
    row, col = (lax.broadcasted_iota(jnp.int32, (total, half), axis) for axis in range(2))
    slot = lax.bitwise_and(row, PADDED - 1)
    source = lax.shift_right_logical(row, 4) * capacity + slot
    side = lax.bitwise_and(lax.shift_right_logical(row, 3), 1)
    found = (source == col) & (slot < capacity)
    parts = [
        dot_plain(jnp.where(found & (side == k), 1.0, 0.0).astype(jnp.bfloat16), rows)
        for k, rows in enumerate((mine_ref[:half, :], other_ref[...]))
    ]
    out_ref[...] = (parts[0] + parts[1]).astype(jnp.bfloat16)


def spread(mine, other, columns, capacity):
    return pl.pallas_call(
        functools.partial(spread_kernel, capacity),
        out_shape=jax.ShapeDtypeStruct((columns * 2 * PADDED, mine.shape[1]), jnp.bfloat16),
        compiler_params=pltpu.CompilerParams(vmem_limit_bytes=24 << 20),
        name="spread_rows",
    )(mine, other)


def prepare_kernel(tokens_ref, routes_ref, combine_ref, cot_ref, own_ref, send_ref, chosen_ref):
    count = tokens_ref.shape[0]
    square = (count, count)
    row, col = lax.broadcasted_iota(jnp.int32, square, 0), lax.broadcasted_iota(jnp.int32, square, 1)
    chosen = routes_ref[...].astype(jnp.float32)
    down = [jnp.broadcast_to(chosen[:, k : k + 1], square) for k in range(2)]
    across = [expert.T for expert in down]
    slots = [
        jnp.sum(
            jnp.where((row < col) & ((down[0] == expert) | (down[1] == expert)), 1.0, 0.0),
            axis=0,
            keepdims=True,
        )
        for expert in across
    ]
    own_ref[:count, :] = tokens_ref[...]
    own_ref[count:, :] = jnp.zeros((own_ref.shape[0] - count, own_ref.shape[1]), jnp.bfloat16)
    lines = [across[0][:1], across[1][:1], slots[0], slots[1], jnp.zeros((INFO - 4, count), jnp.float32)]
    own_ref[count:, :count] = jnp.concatenate(lines, axis=0).astype(jnp.bfloat16)
    cot = cot_ref[...].astype(jnp.float32)
    total = None
    for k in range(2):
        expert, slot = across[k][:1].astype(jnp.int32), slots[k].astype(jnp.int32)
        chosen_ref[k : k + 1, :] = expert
        chosen_ref[k + 2 : k + 3, :] = slot
        quarter, last = lax.shift_right_logical(expert, 2), lax.bitwise_and(expert, 1)
        pair = lax.bitwise_and(lax.shift_right_logical(expert, 1), 1)
        places = ((quarter * 2 + last) * 2 + pair) * PADDED + slot
        places = jnp.broadcast_to(places, (send_ref.shape[0], count))
        pick = jnp.where(lax.broadcasted_iota(jnp.int32, places.shape, 0) == places, 1.0, 0.0)
        weighted = (combine_ref[:, k : k + 1] * cot).astype(jnp.bfloat16)
        part = dot_plain(pick.astype(jnp.bfloat16), weighted)
        total = part if total is None else total + part
    send_ref[...] = total.astype(jnp.bfloat16)


def prepare(tokens, routes, combine, cotangent, experts):
    count, width = tokens.shape
    return pl.pallas_call(
        prepare_kernel,
        out_shape=[
            jax.ShapeDtypeStruct((count + INFO, width), jnp.bfloat16),
            jax.ShapeDtypeStruct((experts * PADDED, width), jnp.bfloat16),
            jax.ShapeDtypeStruct((4, count), jnp.int32),
        ],
        compiler_params=pltpu.CompilerParams(vmem_limit_bytes=24 << 20),
        name="prepare_rows",
    )(tokens, routes, combine, cotangent)


def column_of(expert):
    return expert // 4 * 2 + expert % 2


def pair_of(expert):
    return expert // 2 % 2


def ring_shift(x, step):
    groups, experts = lax.axis_size("dp"), lax.axis_size("expert")
    pairs = []
    for group in range(groups):
        for expert in range(experts):
            z = (group * 2 + pair_of(expert) + step) % (2 * groups)
            target = z // 2 * experts + expert // 4 * 4 + z % 2 * 2 + expert % 2
            pairs.append((group * experts + expert, target))
    return lax.ppermute(x, ("dp", "expert"), pairs)


def group_shift(x, step):
    groups = lax.axis_size("dp")
    return lax.ppermute(x, "dp", [(g, (g + step) % groups) for g in range(groups)])


def pair_swap(x):
    experts = lax.axis_size("expert")
    return lax.ppermute(x, "expert", [(e, e + 2 - pair_of(e) * 4) for e in range(experts)])


def sum_of(*parts):
    total = parts[0].astype(jnp.float32)
    for part in parts[1:]:
        total = total + part.astype(jnp.float32)
    return total.astype(jnp.bfloat16)


def join(size, blocks):
    whole = jnp.zeros((size, blocks[0][1].shape[1]), blocks[0][1].dtype)
    for start, block in blocks:
        whole = lax.dynamic_update_slice_in_dim(whole, block, start, 0)
    return whole


def on_device(tokens, routes, combine, w_gate, w_up, w_down, cotangent):
    experts = lax.axis_size("expert")
    groups = lax.axis_size("dp")
    count = tokens.shape[0]
    width = tokens.shape[1]
    capacity = 10 * count // (4 * experts)
    slot_total = experts * capacity
    row_total = groups * slot_total
    columns = experts // 2
    planes = 2 * groups
    column_groups = [[e for e in range(experts) if pair_of(e) == pair] for pair in range(2)]
    ring_groups = [
        [g * experts + column // 2 * 4 + pair * 2 + column % 2 for g in range(groups) for pair in range(2)]
        for column in range(columns)
    ]
    everyone = ("dp", "expert")
    group = lax.axis_index("dp")
    place = lax.axis_index("expert")
    z = group * 2 + pair_of(place)

    own, send_cot, chosen = prepare(tokens, routes, combine, cotangent, experts)
    pair = pair_of(place)
    got = lax.all_to_all(
        send_cot.reshape(columns, 2 * PADDED, width),
        "expert",
        split_axis=0,
        concat_axis=0,
        tiled=True,
        axis_index_groups=column_groups,
    )
    got = [got[:, k * PADDED : k * PADDED + capacity].reshape(slot_total // 2, width) for k in range(2)]
    kept, passed = jnp.where(pair == 0, got[0], got[1]), jnp.where(pair == 0, got[1], got[0])
    got_cot = jnp.concatenate([kept, pair_swap(passed)], axis=0)
    cot = cotangent.astype(jnp.float32)
    target_row = (column_of(chosen[:2]) * 2 + (pair_of(chosen[:2]) != pair)) * PADDED + chosen[2:]
    positions = jnp.arange(columns * 2 * PADDED, dtype=jnp.int32)[:, None]
    pick_first = (positions == target_row[0:1]).astype(jnp.bfloat16)
    pick_second = (positions == target_row[1:2]).astype(jnp.bfloat16)

    held_count = count + INFO
    ring = lax.all_gather(own, everyone, axis_index_groups=ring_groups, axis=0, tiled=True)

    half_rows = slot_total // 2
    cot_rows = lax.all_gather(got_cot, "dp", axis=0, tiled=True)

    held = ring.reshape(planes, held_count, width)[:, count : count + 4, :count].astype(jnp.int32)
    block = jnp.arange(planes, dtype=jnp.int32)[:, None, None]
    ring_expert, ring_slot = held[:, 0:2], held[:, 2:4]
    ring_row = column_of(ring_expert) * (planes * capacity) + block * capacity + ring_slot
    here = pair_of(ring_expert) == pair_of(place)
    ring_row = jnp.where(here, ring_row, -1)
    held_row = jnp.pad(ring_row, ((0, 0), (0, 0), (0, held_count - count)), constant_values=-1)
    held_row = held_row.transpose(1, 0, 2).reshape(2, 1, planes * held_count)
    row_ids = jnp.arange(row_total, dtype=jnp.int32)[:, None]
    select = ((row_ids == held_row[0]) | (row_ids == held_row[1])).astype(jnp.bfloat16)
    send_tokens = dot_plain(select, ring).astype(jnp.bfloat16)
    token_rows = lax.all_to_all(
        send_tokens.reshape(columns, planes * capacity, width),
        "expert",
        split_axis=0,
        concat_axis=0,
        tiled=True,
        axis_index_groups=column_groups,
    ).reshape(row_total, width)

    ids = jnp.arange(row_total, dtype=jnp.int32)
    column, plane, slot = ids // (planes * capacity), ids // capacity % planes, ids % capacity
    cot_place = (plane // 2 * 2 + (plane % 2 != pair)) * (slot_total // 2) + column * capacity + slot
    side = ids // half_rows % 2
    out_plane = ids // slot_total * 2 + jnp.where(side == 1, 1 - pair, pair)
    out_place = (ids % half_rows // capacity * planes + out_plane) * capacity + ids % capacity

    down_w = w_down[0]
    up_gate_w = jnp.concatenate([w_gate[0], w_up[0]], axis=1)
    up_gate_wt = jnp.concatenate([w_gate[0].T, w_up[0].T], axis=0)
    pre, hidden = forward(token_rows, up_gate_w)
    hidden_cot, part_out = outward(out_place[:, None], hidden, down_w)
    expert_out = lax.psum_scatter(part_out, "dp", scatter_dimension=0, tiled=True)

    d_hidden = dot_last(cot_rows, down_w).astype(jnp.bfloat16)
    d_hidden, _ = lax.optimization_barrier((d_hidden, part_out))
    d_both, back_rows = backward(cot_place[:, None], d_hidden, pre, up_gate_wt)
    d_gate, d_up = d_both[:, : down_w.shape[0]], d_both[:, down_w.shape[0] :]
    arrived = lax.all_to_all(
        back_rows.reshape(columns, planes * capacity, width),
        "expert",
        split_axis=0,
        concat_axis=0,
        tiled=True,
        axis_index_groups=column_groups,
    ).reshape(row_total, width)
    token_row = ring_row.transpose(1, 0, 2).reshape(2, planes * count, 1)
    add_up = ((token_row[0] == ids[None, :]) | (token_row[1] == ids[None, :])).astype(jnp.bfloat16)
    d_ring = dot_plain(add_up, arrived).astype(jnp.bfloat16)
    d_tokens = lax.psum_scatter(
        d_ring, everyone, axis_index_groups=ring_groups, scatter_dimension=0, tiled=True
    )

    returned = lax.all_to_all(
        spread(expert_out, pair_swap(expert_out[half_rows:]), columns, capacity).reshape(columns, 2 * PADDED, width),
        "expert",
        split_axis=0,
        concat_axis=0,
        tiled=True,
        axis_index_groups=column_groups,
    ).reshape(columns * 2 * PADDED, width)
    first_out = dot_first(pick_first, returned)
    second_out = dot_first(pick_second, returned)
    out = (combine[:, 0:1] * first_out + combine[:, 1:2] * second_out).astype(jnp.bfloat16)
    d_combine = jnp.stack(
        [jnp.sum(cot * first_out, axis=1), jnp.sum(cot * second_out, axis=1)], axis=1
    )

    grad_gate = dot_first(token_rows, d_gate).astype(jnp.bfloat16)
    grad_up = dot_first(token_rows, d_up).astype(jnp.bfloat16)
    grad_down = dot_first(hidden_cot, cot_rows).astype(jnp.bfloat16)
    return (out, d_tokens, d_combine, grad_gate[None], grad_up[None], grad_down[None])


def solution(mesh):
    placed = (
        P(("dp", "expert"), None),
        P(("dp", "expert"), None),
        P(("dp", "expert"), None),
        P("expert", None, "dp"),
        P("expert", None, "dp"),
        P("expert", "dp", None),
        P(("dp", "expert"), None),
    )
    return jax.shard_map(
        on_device,
        mesh=mesh,
        in_specs=placed,
        out_specs=(
            P(("dp", "expert"), None),
            P(("dp", "expert"), None),
            P(("dp", "expert"), None),
            P("expert", None, "dp"),
            P("expert", None, "dp"),
            P("expert", "dp", None),
        ),
        check_vma=False,
    )
```

```python
import functools
import jax
import jax.numpy as jnp
from jax import lax
from jax.experimental import pallas as pl
from jax.experimental.pallas import tpu as pltpu
from jax.sharding import PartitionSpec as P


def dot_plain(left, right):
    return jnp.dot(left, right, preferred_element_type=jnp.float32)


def dot_last(left, right):
    return lax.dot_general(
        left, right, (((1,), (1,)), ((), ())), preferred_element_type=jnp.float32
    )


def dot_first(left, right):
    return lax.dot_general(
        left, right, (((0,), (0,)), ((), ())), preferred_element_type=jnp.float32
    )


ROWS = 256


def select_kernel(code_ref, x_ref, out_ref):
    row = pl.program_id(0) * ROWS + lax.broadcasted_iota(jnp.int32, (ROWS, x_ref.shape[0]), 0)
    found = (row == code_ref[:1]) | (row == code_ref[1:])
    select = jnp.where(found, 1.0, 0.0).astype(jnp.bfloat16)
    out_ref[...] = dot_plain(select, x_ref[...]).astype(jnp.bfloat16)


def select_rows(codes, x, total):
    held, width = x.shape
    return pl.pallas_call(
        select_kernel,
        grid=(total // ROWS,),
        in_specs=[
            pl.BlockSpec((2, held), lambda i: (0, 0), pipeline_mode=pl.Buffered(1)),
            pl.BlockSpec((held, width), lambda i: (0, 0), pipeline_mode=pl.Buffered(1)),
        ],
        out_specs=pl.BlockSpec((ROWS, width), lambda i: (i, 0)),
        out_shape=pltpu.HBM((total, width), jnp.bfloat16),
        compiler_params=pltpu.CompilerParams(vmem_limit_bytes=24 << 20),
        name="select_rows",
    )(codes, x)


def forward_kernel(x_ref, w_ref, pre_ref, hidden_ref):
    pre = dot_plain(x_ref[...], w_ref[...])
    pre_ref[...] = pre
    half = pre.shape[1] // 2
    gate_pre, up_pre = pre[:, :half], pre[:, half:]
    hidden_ref[...] = (gate_pre * jax.nn.sigmoid(gate_pre) * up_pre).astype(jnp.bfloat16)


def forward(rows, weights):
    total, width = rows.shape
    both = weights.shape[1]
    return pl.pallas_call(
        forward_kernel,
        grid=(total // ROWS,),
        in_specs=[
            pl.BlockSpec((ROWS, width), lambda i: (i, 0)),
            pl.BlockSpec((width, both), lambda i: (0, 0), pipeline_mode=pl.Buffered(1)),
        ],
        out_specs=[
            pl.BlockSpec((ROWS, both), lambda i: (i, 0)),
            pl.BlockSpec((ROWS, both // 2), lambda i: (i, 0)),
        ],
        out_shape=[
            pltpu.HBM((total, both), jnp.float32),
            jax.ShapeDtypeStruct((total, both // 2), jnp.bfloat16),
        ],
        compiler_params=pltpu.CompilerParams(vmem_limit_bytes=24 << 20),
        name="forward_rows",
    )(rows, weights)


def backward_kernel(place_ref, d_ref, pre_ref, w_ref, grads_ref, back_ref):
    total = d_ref.shape[0]
    places = jnp.broadcast_to(place_ref[...], (ROWS, total))
    select = jnp.where(places == lax.broadcasted_iota(jnp.int32, (ROWS, total), 1), 1.0, 0.0)
    d_hidden = dot_plain(select.astype(jnp.bfloat16), d_ref[...])
    half = d_hidden.shape[1]
    gate_pre, up_pre = pre_ref[:, :half], pre_ref[:, half:]
    sigmoid_gate = jax.nn.sigmoid(gate_pre)
    d_gate = d_hidden * up_pre * sigmoid_gate * (1.0 + gate_pre * (1.0 - sigmoid_gate))
    d_up = d_hidden * gate_pre * sigmoid_gate
    grads_ref[:, :half] = d_gate.astype(jnp.bfloat16)
    grads_ref[:, half:] = d_up.astype(jnp.bfloat16)
    back_ref[...] = dot_plain(grads_ref[...], w_ref[...]).astype(jnp.bfloat16)


def backward(places, d_hidden, pre, weights):
    total, both = pre.shape
    width = weights.shape[1]
    return pl.pallas_call(
        backward_kernel,
        grid=(total // ROWS,),
        in_specs=[
            pl.BlockSpec((ROWS, 1), lambda i: (i, 0)),
            pl.BlockSpec((total, both // 2), lambda i: (0, 0), pipeline_mode=pl.Buffered(1)),
            pl.BlockSpec((ROWS, both), lambda i: (i, 0)),
            pl.BlockSpec((both, width), lambda i: (0, 0), pipeline_mode=pl.Buffered(1)),
        ],
        out_specs=[
            pl.BlockSpec((ROWS, both), lambda i: (i, 0)),
            pl.BlockSpec((ROWS, width), lambda i: (i, 0)),
        ],
        out_shape=[
            pltpu.HBM((total, both), jnp.bfloat16),
            pltpu.HBM((total, width), jnp.bfloat16),
        ],
        compiler_params=pltpu.CompilerParams(vmem_limit_bytes=24 << 20),
        name="backward_rows",
    )(places, d_hidden, pre, weights)


def outward_kernel(place_ref, hidden_ref, w_ref, hidden_out_ref, out_ref):
    total = hidden_ref.shape[0]
    places = jnp.broadcast_to(place_ref[...], (ROWS, total))
    select = jnp.where(places == lax.broadcasted_iota(jnp.int32, (ROWS, total), 1), 1.0, 0.0)
    hidden = dot_plain(select.astype(jnp.bfloat16), hidden_ref[...]).astype(jnp.bfloat16)
    hidden_out_ref[...] = hidden
    out_ref[...] = dot_plain(hidden, w_ref[...]).astype(jnp.bfloat16)


def outward(places, hidden, weights):
    total, part = hidden.shape
    width = weights.shape[1]
    return pl.pallas_call(
        outward_kernel,
        grid=(total // ROWS,),
        in_specs=[
            pl.BlockSpec((ROWS, 1), lambda i: (i, 0)),
            pl.BlockSpec((total, part), lambda i: (0, 0), pipeline_mode=pl.Buffered(1)),
            pl.BlockSpec((part, width), lambda i: (0, 0), pipeline_mode=pl.Buffered(1)),
        ],
        out_specs=[
            pl.BlockSpec((ROWS, part), lambda i: (i, 0)),
            pl.BlockSpec((ROWS, width), lambda i: (i, 0)),
        ],
        out_shape=[
            jax.ShapeDtypeStruct((total, part), jnp.bfloat16),
            pltpu.HBM((total, width), jnp.bfloat16),
        ],
        compiler_params=pltpu.CompilerParams(vmem_limit_bytes=24 << 20),
        name="outward_rows",
    )(places, hidden, weights)


PADDED = 8
INFO = 8


def spread_kernel(capacity, mine_ref, other_ref, out_ref):
    half, total = other_ref.shape[0], out_ref.shape[0]
    row, col = (lax.broadcasted_iota(jnp.int32, (total, half), axis) for axis in range(2))
    slot = lax.bitwise_and(row, PADDED - 1)
    source = lax.shift_right_logical(row, 4) * capacity + slot
    side = lax.bitwise_and(lax.shift_right_logical(row, 3), 1)
    found = (source == col) & (slot < capacity)
    parts = [
        dot_plain(jnp.where(found & (side == k), 1.0, 0.0).astype(jnp.bfloat16), rows)
        for k, rows in enumerate((mine_ref[:half, :], other_ref[...]))
    ]
    out_ref[...] = (parts[0] + parts[1]).astype(jnp.bfloat16)


def spread(mine, other, columns, capacity):
    return pl.pallas_call(
        functools.partial(spread_kernel, capacity),
        out_shape=jax.ShapeDtypeStruct((columns * 2 * PADDED, mine.shape[1]), jnp.bfloat16),
        compiler_params=pltpu.CompilerParams(vmem_limit_bytes=24 << 20),
        name="spread_rows",
    )(mine, other)


def prepare_kernel(tokens_ref, routes_ref, combine_ref, cot_ref, own_ref, send_ref, chosen_ref):
    count = tokens_ref.shape[0]
    square = (count, count)
    row, col = lax.broadcasted_iota(jnp.int32, square, 0), lax.broadcasted_iota(jnp.int32, square, 1)
    chosen = routes_ref[...].astype(jnp.float32)
    across = [jnp.broadcast_to(chosen[k : k + 1], square) for k in range(2)]
    down = [expert.T for expert in across]
    slots = [
        jnp.sum(
            jnp.where((row < col) & ((down[0] == expert) | (down[1] == expert)), 1.0, 0.0),
            axis=0,
            keepdims=True,
        )
        for expert in across
    ]
    own_ref[:count, :] = tokens_ref[...]
    own_ref[count:, :] = jnp.zeros((own_ref.shape[0] - count, own_ref.shape[1]), jnp.bfloat16)
    lines = [across[0][:1], across[1][:1], slots[0], slots[1], jnp.zeros((INFO - 4, count), jnp.float32)]
    own_ref[count:, :count] = jnp.concatenate(lines, axis=0).astype(jnp.bfloat16)
    cot = cot_ref[...].astype(jnp.float32)
    total = None
    for k in range(2):
        expert, slot = across[k][:1].astype(jnp.int32), slots[k].astype(jnp.int32)
        chosen_ref[k : k + 1, :] = expert
        chosen_ref[k + 2 : k + 3, :] = slot
        quarter, last = lax.shift_right_logical(expert, 2), lax.bitwise_and(expert, 1)
        pair = lax.bitwise_and(lax.shift_right_logical(expert, 1), 1)
        places = ((quarter * 2 + last) * 2 + pair) * PADDED + slot
        places = jnp.broadcast_to(places, (send_ref.shape[0], count))
        pick = jnp.where(lax.broadcasted_iota(jnp.int32, places.shape, 0) == places, 1.0, 0.0)
        weight = jnp.broadcast_to(combine_ref[k : k + 1], square).T[:, :1]
        weighted = (weight * cot).astype(jnp.bfloat16)
        part = dot_plain(pick.astype(jnp.bfloat16), weighted)
        total = part if total is None else total + part
    send_ref[...] = total.astype(jnp.bfloat16)


def prepare(tokens, routes, combine, cotangent, experts):
    count, width = tokens.shape
    return pl.pallas_call(
        prepare_kernel,
        out_shape=[
            jax.ShapeDtypeStruct((count + INFO, width), jnp.bfloat16),
            jax.ShapeDtypeStruct((experts * PADDED, width), jnp.bfloat16),
            jax.ShapeDtypeStruct((4, count), jnp.int32),
        ],
        compiler_params=pltpu.CompilerParams(vmem_limit_bytes=24 << 20),
        name="prepare_rows",
    )(tokens, routes, combine, cotangent)


def column_of(expert):
    return expert // 4 * 2 + expert % 2


def pair_of(expert):
    return expert // 2 % 2


def ring_shift(x, step):
    groups, experts = lax.axis_size("dp"), lax.axis_size("expert")
    pairs = []
    for group in range(groups):
        for expert in range(experts):
            z = (group * 2 + pair_of(expert) + step) % (2 * groups)
            target = z // 2 * experts + expert // 4 * 4 + z % 2 * 2 + expert % 2
            pairs.append((group * experts + expert, target))
    return lax.ppermute(x, ("dp", "expert"), pairs)


def group_shift(x, step):
    groups = lax.axis_size("dp")
    return lax.ppermute(x, "dp", [(g, (g + step) % groups) for g in range(groups)])


def pair_swap(x):
    experts = lax.axis_size("expert")
    return lax.ppermute(x, "expert", [(e, e + 2 - pair_of(e) * 4) for e in range(experts)])


def sum_of(*parts):
    total = parts[0].astype(jnp.float32)
    for part in parts[1:]:
        total = total + part.astype(jnp.float32)
    return total.astype(jnp.bfloat16)


def join(size, blocks):
    whole = jnp.zeros((size, blocks[0][1].shape[1]), blocks[0][1].dtype)
    for start, block in blocks:
        whole = lax.dynamic_update_slice_in_dim(whole, block, start, 0)
    return whole


def on_device(tokens, routes, combine, w_gate, w_up, w_down, cotangent):
    experts = lax.axis_size("expert")
    groups = lax.axis_size("dp")
    count = tokens.shape[0]
    width = tokens.shape[1]
    capacity = 10 * count // (4 * experts)
    slot_total = experts * capacity
    row_total = groups * slot_total
    columns = experts // 2
    planes = 2 * groups
    column_groups = [[e for e in range(experts) if pair_of(e) == pair] for pair in range(2)]
    ring_groups = [
        [g * experts + column // 2 * 4 + pair * 2 + column % 2 for g in range(groups) for pair in range(2)]
        for column in range(columns)
    ]
    everyone = ("dp", "expert")
    group = lax.axis_index("dp")
    place = lax.axis_index("expert")
    z = group * 2 + pair_of(place)

    own, send_cot, chosen = prepare(tokens, routes.T, combine.T, cotangent, experts)
    pair = pair_of(place)
    got = lax.all_to_all(
        send_cot.reshape(columns, 2 * PADDED, width),
        "expert",
        split_axis=0,
        concat_axis=0,
        tiled=True,
        axis_index_groups=column_groups,
    )
    got = [got[:, k * PADDED : k * PADDED + capacity].reshape(slot_total // 2, width) for k in range(2)]
    kept, passed = jnp.where(pair == 0, got[0], got[1]), jnp.where(pair == 0, got[1], got[0])
    got_cot = jnp.concatenate([kept, pair_swap(passed)], axis=0)
    cot = cotangent.astype(jnp.float32)
    target_row = (column_of(chosen[:2]) * 2 + (pair_of(chosen[:2]) != pair)) * PADDED + chosen[2:]
    positions = jnp.arange(columns * 2 * PADDED, dtype=jnp.int32)[:, None]
    pick_first = (positions == target_row[0:1]).astype(jnp.bfloat16)
    pick_second = (positions == target_row[1:2]).astype(jnp.bfloat16)

    held_count = count + INFO
    ring = lax.all_gather(own, everyone, axis_index_groups=ring_groups, axis=0, tiled=True)

    half_rows = slot_total // 2
    cot_rows = lax.all_gather(got_cot, "dp", axis=0, tiled=True)

    held = ring.reshape(planes, held_count, width)[:, count : count + 4, :count].astype(jnp.int32)
    block = jnp.arange(planes, dtype=jnp.int32)[:, None, None]
    ring_expert, ring_slot = held[:, 0:2], held[:, 2:4]
    ring_row = column_of(ring_expert) * (planes * capacity) + block * capacity + ring_slot
    here = pair_of(ring_expert) == pair_of(place)
    ring_row = jnp.where(here, ring_row, -1)
    held_row = jnp.pad(ring_row, ((0, 0), (0, 0), (0, held_count - count)), constant_values=-1)
    held_row = held_row.transpose(1, 0, 2).reshape(2, planes * held_count)
    send_tokens = select_rows(held_row, ring, row_total)
    token_rows = lax.all_to_all(
        send_tokens.reshape(columns, planes * capacity, width),
        "expert",
        split_axis=0,
        concat_axis=0,
        tiled=True,
        axis_index_groups=column_groups,
    ).reshape(row_total, width)

    ids = jnp.arange(row_total, dtype=jnp.int32)
    column, plane, slot = ids // (planes * capacity), ids // capacity % planes, ids % capacity
    cot_place = (plane // 2 * 2 + (plane % 2 != pair)) * (slot_total // 2) + column * capacity + slot
    side = ids // half_rows % 2
    out_plane = ids // slot_total * 2 + jnp.where(side == 1, 1 - pair, pair)
    out_place = (ids % half_rows // capacity * planes + out_plane) * capacity + ids % capacity

    down_w = w_down[0]
    up_gate_w = jnp.concatenate([w_gate[0], w_up[0]], axis=1)
    up_gate_wt = jnp.concatenate([w_gate[0].T, w_up[0].T], axis=0)
    pre, hidden = forward(token_rows, up_gate_w)
    hidden_cot, part_out = outward(out_place[:, None], hidden, down_w)
    expert_out = lax.psum_scatter(part_out, "dp", scatter_dimension=0, tiled=True)

    d_hidden = dot_last(cot_rows, down_w).astype(jnp.bfloat16)
    d_hidden, _ = lax.optimization_barrier((d_hidden, part_out))
    d_both, back_rows = backward(cot_place[:, None], d_hidden, pre, up_gate_wt)
    d_gate, d_up = d_both[:, : down_w.shape[0]], d_both[:, down_w.shape[0] :]
    arrived = lax.all_to_all(
        back_rows.reshape(columns, planes * capacity, width),
        "expert",
        split_axis=0,
        concat_axis=0,
        tiled=True,
        axis_index_groups=column_groups,
    ).reshape(row_total, width)
    token_row = ring_row.transpose(1, 0, 2).reshape(2, planes * count, 1)
    add_up = ((token_row[0] == ids[None, :]) | (token_row[1] == ids[None, :])).astype(jnp.bfloat16)
    d_ring = dot_plain(add_up, arrived).astype(jnp.bfloat16)
    d_tokens = lax.psum_scatter(
        d_ring, everyone, axis_index_groups=ring_groups, scatter_dimension=0, tiled=True
    )

    returned = lax.all_to_all(
        spread(expert_out, pair_swap(expert_out[half_rows:]), columns, capacity).reshape(columns, 2 * PADDED, width),
        "expert",
        split_axis=0,
        concat_axis=0,
        tiled=True,
        axis_index_groups=column_groups,
    ).reshape(columns * 2 * PADDED, width)
    first_out = dot_first(pick_first, returned)
    second_out = dot_first(pick_second, returned)
    out = (combine[:, 0:1] * first_out + combine[:, 1:2] * second_out).astype(jnp.bfloat16)
    d_combine = jnp.stack(
        [jnp.sum(cot * first_out, axis=1), jnp.sum(cot * second_out, axis=1)], axis=1
    )

    grad_gate = dot_first(token_rows, d_gate).astype(jnp.bfloat16)
    grad_up = dot_first(token_rows, d_up).astype(jnp.bfloat16)
    grad_down = dot_first(hidden_cot, cot_rows).astype(jnp.bfloat16)
    return (out, d_tokens, d_combine, grad_gate[None], grad_up[None], grad_down[None])


def solution(mesh):
    placed = (
        P(("dp", "expert"), None),
        P(("dp", "expert"), None),
        P(("dp", "expert"), None),
        P("expert", None, "dp"),
        P("expert", None, "dp"),
        P("expert", "dp", None),
        P(("dp", "expert"), None),
    )
    return jax.shard_map(
        on_device,
        mesh=mesh,
        in_specs=placed,
        out_specs=(
            P(("dp", "expert"), None),
            P(("dp", "expert"), None),
            P(("dp", "expert"), None),
            P("expert", None, "dp"),
            P("expert", None, "dp"),
            P("expert", "dp", None),
        ),
        check_vma=False,
    )
```

```python
import functools
import jax
import jax.numpy as jnp
from jax import lax
from jax.experimental import pallas as pl
from jax.experimental.pallas import tpu as pltpu
from jax.sharding import PartitionSpec as P


def dot_plain(left, right):
    return jnp.dot(left, right, preferred_element_type=jnp.float32)


def dot_last(left, right):
    return lax.dot_general(
        left, right, (((1,), (1,)), ((), ())), preferred_element_type=jnp.float32
    )


def dot_first(left, right):
    return lax.dot_general(
        left, right, (((0,), (0,)), ((), ())), preferred_element_type=jnp.float32
    )


ROWS = 256


def select_kernel(code_ref, x_ref, out_ref):
    row = pl.program_id(0) * ROWS + lax.broadcasted_iota(jnp.int32, (ROWS, x_ref.shape[0]), 0)
    found = (row == code_ref[:1]) | (row == code_ref[1:])
    select = jnp.where(found, 1.0, 0.0).astype(jnp.bfloat16)
    out_ref[...] = dot_plain(select, x_ref[...]).astype(jnp.bfloat16)


def select_rows(codes, x, total):
    held, width = x.shape
    return pl.pallas_call(
        select_kernel,
        grid=(total // ROWS,),
        in_specs=[
            pl.BlockSpec((2, held), lambda i: (0, 0), pipeline_mode=pl.Buffered(1)),
            pl.BlockSpec((held, width), lambda i: (0, 0), pipeline_mode=pl.Buffered(1)),
        ],
        out_specs=pl.BlockSpec((ROWS, width), lambda i: (i, 0)),
        out_shape=pltpu.HBM((total, width), jnp.bfloat16),
        compiler_params=pltpu.CompilerParams(vmem_limit_bytes=24 << 20),
        name="select_rows",
    )(codes, pltpu.with_memory_space_constraint(x, pltpu.HBM))


def forward_kernel(x_ref, w_ref, hidden_ref):
    pre = dot_plain(x_ref[...], w_ref[...])
    half = pre.shape[1] // 2
    gate_pre, up_pre = pre[:, :half], pre[:, half:]
    hidden_ref[...] = (gate_pre * jax.nn.sigmoid(gate_pre) * up_pre).astype(jnp.bfloat16)


def forward(rows, weights):
    total, width = rows.shape
    both = weights.shape[1]
    return pl.pallas_call(
        forward_kernel,
        grid=(total // ROWS,),
        in_specs=[
            pl.BlockSpec((ROWS, width), lambda i: (i, 0)),
            pl.BlockSpec((width, both), lambda i: (0, 0), pipeline_mode=pl.Buffered(1)),
        ],
        out_specs=pl.BlockSpec((ROWS, both // 2), lambda i: (i, 0)),
        out_shape=jax.ShapeDtypeStruct((total, both // 2), jnp.bfloat16),
        compiler_params=pltpu.CompilerParams(vmem_limit_bytes=24 << 20),
        name="forward_rows",
    )(rows, weights)


def backward_kernel(place_ref, d_ref, x_ref, w_ref, wt_ref, grads_ref, back_ref):
    total = d_ref.shape[0]
    places = jnp.broadcast_to(place_ref[...], (ROWS, total))
    select = jnp.where(places == lax.broadcasted_iota(jnp.int32, (ROWS, total), 1), 1.0, 0.0)
    d_hidden = dot_plain(select.astype(jnp.bfloat16), d_ref[...])
    half = d_hidden.shape[1]
    pre = dot_plain(x_ref[...], w_ref[...])
    gate_pre, up_pre = pre[:, :half], pre[:, half:]
    sigmoid_gate = jax.nn.sigmoid(gate_pre)
    d_gate = d_hidden * up_pre * sigmoid_gate * (1.0 + gate_pre * (1.0 - sigmoid_gate))
    d_up = d_hidden * gate_pre * sigmoid_gate
    grads_ref[:, :half] = d_gate.astype(jnp.bfloat16)
    grads_ref[:, half:] = d_up.astype(jnp.bfloat16)
    back_ref[...] = dot_plain(grads_ref[...], wt_ref[...]).astype(jnp.bfloat16)


def backward(places, d_hidden, rows, weights, weights_t):
    total, width = rows.shape
    both = weights.shape[1]
    return pl.pallas_call(
        backward_kernel,
        grid=(total // ROWS,),
        in_specs=[
            pl.BlockSpec((ROWS, 1), lambda i: (i, 0)),
            pl.BlockSpec((total, both // 2), lambda i: (0, 0), pipeline_mode=pl.Buffered(1)),
            pl.BlockSpec((ROWS, width), lambda i: (i, 0)),
            pl.BlockSpec((width, both), lambda i: (0, 0), pipeline_mode=pl.Buffered(1)),
            pl.BlockSpec((both, width), lambda i: (0, 0), pipeline_mode=pl.Buffered(1)),
        ],
        out_specs=[
            pl.BlockSpec((ROWS, both), lambda i: (i, 0)),
            pl.BlockSpec((ROWS, width), lambda i: (i, 0)),
        ],
        out_shape=[
            pltpu.HBM((total, both), jnp.bfloat16),
            pltpu.HBM((total, width), jnp.bfloat16),
        ],
        compiler_params=pltpu.CompilerParams(vmem_limit_bytes=24 << 20),
        name="backward_rows",
    )(places, d_hidden, rows, weights, weights_t)


def outward_kernel(place_ref, hidden_ref, w_ref, hidden_out_ref, out_ref):
    total = hidden_ref.shape[0]
    places = jnp.broadcast_to(place_ref[...], (ROWS, total))
    select = jnp.where(places == lax.broadcasted_iota(jnp.int32, (ROWS, total), 1), 1.0, 0.0)
    hidden = dot_plain(select.astype(jnp.bfloat16), hidden_ref[...]).astype(jnp.bfloat16)
    hidden_out_ref[...] = hidden
    out_ref[...] = dot_plain(hidden, w_ref[...]).astype(jnp.bfloat16)


def outward(places, hidden, weights):
    total, part = hidden.shape
    width = weights.shape[1]
    return pl.pallas_call(
        outward_kernel,
        grid=(total // ROWS,),
        in_specs=[
            pl.BlockSpec((ROWS, 1), lambda i: (i, 0)),
            pl.BlockSpec((total, part), lambda i: (0, 0), pipeline_mode=pl.Buffered(1)),
            pl.BlockSpec((part, width), lambda i: (0, 0), pipeline_mode=pl.Buffered(1)),
        ],
        out_specs=[
            pl.BlockSpec((ROWS, part), lambda i: (i, 0)),
            pl.BlockSpec((ROWS, width), lambda i: (i, 0)),
        ],
        out_shape=[
            jax.ShapeDtypeStruct((total, part), jnp.bfloat16),
            pltpu.HBM((total, width), jnp.bfloat16),
        ],
        compiler_params=pltpu.CompilerParams(vmem_limit_bytes=24 << 20),
        name="outward_rows",
    )(places, hidden, weights)


PADDED = 8
INFO = 8


def spread_kernel(capacity, mine_ref, other_ref, out_ref):
    half, total = other_ref.shape[0], out_ref.shape[0]
    row, col = (lax.broadcasted_iota(jnp.int32, (total, half), axis) for axis in range(2))
    slot = lax.bitwise_and(row, PADDED - 1)
    source = lax.shift_right_logical(row, 4) * capacity + slot
    side = lax.bitwise_and(lax.shift_right_logical(row, 3), 1)
    found = (source == col) & (slot < capacity)
    parts = [
        dot_plain(jnp.where(found & (side == k), 1.0, 0.0).astype(jnp.bfloat16), rows)
        for k, rows in enumerate((mine_ref[:half, :], other_ref[...]))
    ]
    out_ref[...] = (parts[0] + parts[1]).astype(jnp.bfloat16)


def spread(mine, other, columns, capacity):
    return pl.pallas_call(
        functools.partial(spread_kernel, capacity),
        out_shape=jax.ShapeDtypeStruct((columns * 2 * PADDED, mine.shape[1]), jnp.bfloat16),
        compiler_params=pltpu.CompilerParams(vmem_limit_bytes=24 << 20),
        name="spread_rows",
    )(mine, other)


def prepare_kernel(tokens_ref, routes_ref, combine_ref, cot_ref, own_ref, send_ref, chosen_ref):
    count = tokens_ref.shape[0]
    square = (count, count)
    row, col = lax.broadcasted_iota(jnp.int32, square, 0), lax.broadcasted_iota(jnp.int32, square, 1)
    chosen = routes_ref[...].astype(jnp.float32)
    across = [jnp.broadcast_to(chosen[k : k + 1], square) for k in range(2)]
    down = [expert.T for expert in across]
    slots = [
        jnp.sum(
            jnp.where((row < col) & ((down[0] == expert) | (down[1] == expert)), 1.0, 0.0),
            axis=0,
            keepdims=True,
        )
        for expert in across
    ]
    own_ref[:count, :] = tokens_ref[...]
    own_ref[count:, :] = jnp.zeros((own_ref.shape[0] - count, own_ref.shape[1]), jnp.bfloat16)
    lines = [across[0][:1], across[1][:1], slots[0], slots[1], jnp.zeros((INFO - 4, count), jnp.float32)]
    own_ref[count:, :count] = jnp.concatenate(lines, axis=0).astype(jnp.bfloat16)
    cot = cot_ref[...].astype(jnp.float32)
    total = None
    for k in range(2):
        expert, slot = across[k][:1].astype(jnp.int32), slots[k].astype(jnp.int32)
        chosen_ref[k : k + 1, :] = expert
        chosen_ref[k + 2 : k + 3, :] = slot
        quarter, last = lax.shift_right_logical(expert, 2), lax.bitwise_and(expert, 1)
        pair = lax.bitwise_and(lax.shift_right_logical(expert, 1), 1)
        places = ((quarter * 2 + last) * 2 + pair) * PADDED + slot
        places = jnp.broadcast_to(places, (send_ref.shape[0], count))
        pick = jnp.where(lax.broadcasted_iota(jnp.int32, places.shape, 0) == places, 1.0, 0.0)
        weight = jnp.broadcast_to(combine_ref[k : k + 1], square).T[:, :1]
        weighted = (weight * cot).astype(jnp.bfloat16)
        part = dot_plain(pick.astype(jnp.bfloat16), weighted)
        total = part if total is None else total + part
    send_ref[...] = total.astype(jnp.bfloat16)


def prepare(tokens, routes, combine, cotangent, experts):
    count, width = tokens.shape
    return pl.pallas_call(
        prepare_kernel,
        out_shape=[
            jax.ShapeDtypeStruct((count + INFO, width), jnp.bfloat16),
            jax.ShapeDtypeStruct((experts * PADDED, width), jnp.bfloat16),
            jax.ShapeDtypeStruct((4, count), jnp.int32),
        ],
        compiler_params=pltpu.CompilerParams(vmem_limit_bytes=24 << 20),
        name="prepare_rows",
    )(*(pltpu.with_memory_space_constraint(x, pltpu.HBM) for x in (tokens, routes, combine, cotangent)))


def column_of(expert):
    return expert // 4 * 2 + expert % 2


def pair_of(expert):
    return expert // 2 % 2


def ring_shift(x, step):
    groups, experts = lax.axis_size("dp"), lax.axis_size("expert")
    pairs = []
    for group in range(groups):
        for expert in range(experts):
            z = (group * 2 + pair_of(expert) + step) % (2 * groups)
            target = z // 2 * experts + expert // 4 * 4 + z % 2 * 2 + expert % 2
            pairs.append((group * experts + expert, target))
    return lax.ppermute(x, ("dp", "expert"), pairs)


def group_shift(x, step):
    groups = lax.axis_size("dp")
    return lax.ppermute(x, "dp", [(g, (g + step) % groups) for g in range(groups)])


def pair_swap(x):
    experts = lax.axis_size("expert")
    return lax.ppermute(x, "expert", [(e, e + 2 - pair_of(e) * 4) for e in range(experts)])


def sum_of(*parts):
    total = parts[0].astype(jnp.float32)
    for part in parts[1:]:
        total = total + part.astype(jnp.float32)
    return total.astype(jnp.bfloat16)


def join(size, blocks):
    whole = jnp.zeros((size, blocks[0][1].shape[1]), blocks[0][1].dtype)
    for start, block in blocks:
        whole = lax.dynamic_update_slice_in_dim(whole, block, start, 0)
    return whole


def on_device(tokens, routes, combine, w_gate, w_up, w_down, cotangent):
    experts = lax.axis_size("expert")
    groups = lax.axis_size("dp")
    count = tokens.shape[0]
    width = tokens.shape[1]
    capacity = 10 * count // (4 * experts)
    slot_total = experts * capacity
    row_total = groups * slot_total
    columns = experts // 2
    planes = 2 * groups
    column_groups = [[e for e in range(experts) if pair_of(e) == pair] for pair in range(2)]
    ring_groups = [
        [g * experts + column // 2 * 4 + pair * 2 + column % 2 for g in range(groups) for pair in range(2)]
        for column in range(columns)
    ]
    everyone = ("dp", "expert")
    group = lax.axis_index("dp")
    place = lax.axis_index("expert")
    z = group * 2 + pair_of(place)

    own, send_cot, chosen = prepare(tokens, routes.T, combine.T, cotangent, experts)
    pair = pair_of(place)
    got = lax.all_to_all(
        send_cot.reshape(columns, 2 * PADDED, width),
        "expert",
        split_axis=0,
        concat_axis=0,
        tiled=True,
        axis_index_groups=column_groups,
    )
    got = [got[:, k * PADDED : k * PADDED + capacity].reshape(slot_total // 2, width) for k in range(2)]
    kept, passed = jnp.where(pair == 0, got[0], got[1]), jnp.where(pair == 0, got[1], got[0])
    got_cot = jnp.concatenate([kept, pair_swap(passed)], axis=0)
    cot = cotangent.astype(jnp.float32)
    target_row = (column_of(chosen[:2]) * 2 + (pair_of(chosen[:2]) != pair)) * PADDED + chosen[2:]
    positions = jnp.arange(columns * 2 * PADDED, dtype=jnp.int32)[:, None]
    pick_first = (positions == target_row[0:1]).astype(jnp.bfloat16)
    pick_second = (positions == target_row[1:2]).astype(jnp.bfloat16)

    held_count = count + INFO
    ring = lax.all_gather(own, everyone, axis_index_groups=ring_groups, axis=0, tiled=True)

    half_rows = slot_total // 2
    cot_rows = lax.all_gather(got_cot, "dp", axis=0, tiled=True)

    held = ring.reshape(planes, held_count, width)[:, count : count + 4, :count].astype(jnp.int32)
    block = jnp.arange(planes, dtype=jnp.int32)[:, None, None]
    ring_expert, ring_slot = held[:, 0:2], held[:, 2:4]
    ring_row = column_of(ring_expert) * (planes * capacity) + block * capacity + ring_slot
    here = pair_of(ring_expert) == pair_of(place)
    ring_row = jnp.where(here, ring_row, -1)
    held_row = jnp.pad(ring_row, ((0, 0), (0, 0), (0, held_count - count)), constant_values=-1)
    held_row = held_row.transpose(1, 0, 2).reshape(2, planes * held_count)
    send_tokens = select_rows(held_row, ring, row_total)
    token_rows = lax.all_to_all(
        send_tokens.reshape(columns, planes * capacity, width),
        "expert",
        split_axis=0,
        concat_axis=0,
        tiled=True,
        axis_index_groups=column_groups,
    ).reshape(row_total, width)

    ids = jnp.arange(row_total, dtype=jnp.int32)
    column, plane, slot = ids // (planes * capacity), ids // capacity % planes, ids % capacity
    cot_place = (plane // 2 * 2 + (plane % 2 != pair)) * (slot_total // 2) + column * capacity + slot
    side = ids // half_rows % 2
    out_plane = ids // slot_total * 2 + jnp.where(side == 1, 1 - pair, pair)
    out_place = (ids % half_rows // capacity * planes + out_plane) * capacity + ids % capacity

    down_w = w_down[0]
    up_gate_w = jnp.concatenate([w_gate[0], w_up[0]], axis=1)
    up_gate_wt = jnp.concatenate([w_gate[0].T, w_up[0].T], axis=0)
    hidden = forward(token_rows, up_gate_w)
    hidden_cot, part_out = outward(out_place[:, None], hidden, down_w)
    expert_out = lax.psum_scatter(part_out, "dp", scatter_dimension=0, tiled=True)

    d_hidden = dot_last(cot_rows, down_w).astype(jnp.bfloat16)
    d_hidden, _ = lax.optimization_barrier((d_hidden, part_out))
    d_both, back_rows = backward(cot_place[:, None], d_hidden, token_rows, up_gate_w, up_gate_wt)
    d_gate, d_up = d_both[:, : down_w.shape[0]], d_both[:, down_w.shape[0] :]
    arrived = lax.all_to_all(
        back_rows.reshape(columns, planes * capacity, width),
        "expert",
        split_axis=0,
        concat_axis=0,
        tiled=True,
        axis_index_groups=column_groups,
    ).reshape(row_total, width)
    token_row = ring_row.transpose(1, 0, 2).reshape(2, planes * count, 1)
    add_up = ((token_row[0] == ids[None, :]) | (token_row[1] == ids[None, :])).astype(jnp.bfloat16)
    d_ring = dot_plain(add_up, arrived).astype(jnp.bfloat16)
    d_tokens = lax.psum_scatter(
        d_ring, everyone, axis_index_groups=ring_groups, scatter_dimension=0, tiled=True
    )

    returned = lax.all_to_all(
        spread(expert_out, pair_swap(expert_out[half_rows:]), columns, capacity).reshape(columns, 2 * PADDED, width),
        "expert",
        split_axis=0,
        concat_axis=0,
        tiled=True,
        axis_index_groups=column_groups,
    ).reshape(columns * 2 * PADDED, width)
    first_out = dot_first(pick_first, returned)
    second_out = dot_first(pick_second, returned)
    out = (combine[:, 0:1] * first_out + combine[:, 1:2] * second_out).astype(jnp.bfloat16)
    d_combine = jnp.stack(
        [jnp.sum(cot * first_out, axis=1), jnp.sum(cot * second_out, axis=1)], axis=1
    )

    grad_gate = dot_first(token_rows, d_gate).astype(jnp.bfloat16)
    grad_up = dot_first(token_rows, d_up).astype(jnp.bfloat16)
    grad_down = dot_first(hidden_cot, cot_rows).astype(jnp.bfloat16)
    return (out, d_tokens, d_combine, grad_gate[None], grad_up[None], grad_down[None])


def solution(mesh):
    placed = (
        P(("dp", "expert"), None),
        P(("dp", "expert"), None),
        P(("dp", "expert"), None),
        P("expert", None, "dp"),
        P("expert", None, "dp"),
        P("expert", "dp", None),
        P(("dp", "expert"), None),
    )
    return jax.shard_map(
        on_device,
        mesh=mesh,
        in_specs=placed,
        out_specs=(
            P(("dp", "expert"), None),
            P(("dp", "expert"), None),
            P(("dp", "expert"), None),
            P("expert", None, "dp"),
            P("expert", None, "dp"),
            P("expert", "dp", None),
        ),
        check_vma=False,
    )
```

```python
import functools
import jax
import jax.numpy as jnp
from jax import lax
from jax.experimental import pallas as pl
from jax.experimental.pallas import tpu as pltpu
from jax.sharding import PartitionSpec as P


def dot_plain(left, right):
    return jnp.dot(left, right, preferred_element_type=jnp.float32)


def dot_last(left, right):
    return lax.dot_general(
        left, right, (((1,), (1,)), ((), ())), preferred_element_type=jnp.float32
    )


def dot_first(left, right):
    return lax.dot_general(
        left, right, (((0,), (0,)), ((), ())), preferred_element_type=jnp.float32
    )


ROWS = 256


def select_kernel(code_ref, x_ref, out_ref):
    row = pl.program_id(0) * ROWS + lax.broadcasted_iota(jnp.int32, (ROWS, x_ref.shape[0]), 0)
    found = (row == code_ref[:1]) | (row == code_ref[1:])
    select = jnp.where(found, 1.0, 0.0).astype(jnp.bfloat16)
    out_ref[...] = dot_plain(select, x_ref[...]).astype(jnp.bfloat16)


def select_rows(codes, x, total):
    held, width = x.shape
    return pl.pallas_call(
        select_kernel,
        grid=(total // ROWS,),
        in_specs=[
            pl.BlockSpec((2, held), lambda i: (0, 0), pipeline_mode=pl.Buffered(1)),
            pl.BlockSpec((held, width), lambda i: (0, 0), pipeline_mode=pl.Buffered(1)),
        ],
        out_specs=pl.BlockSpec((ROWS, width), lambda i: (i, 0)),
        out_shape=pltpu.HBM((total, width), jnp.bfloat16),
        compiler_params=pltpu.CompilerParams(vmem_limit_bytes=24 << 20),
        name="select_rows",
    )(codes, x)


def forward_kernel(x_ref, w_ref, pre_ref, hidden_ref):
    pre = dot_plain(x_ref[...], w_ref[...])
    pre_ref[...] = pre
    half = pre.shape[1] // 2
    gate_pre, up_pre = pre[:, :half], pre[:, half:]
    hidden_ref[...] = (gate_pre * jax.nn.sigmoid(gate_pre) * up_pre).astype(jnp.bfloat16)


def forward(rows, weights):
    total, width = rows.shape
    both = weights.shape[1]
    return pl.pallas_call(
        forward_kernel,
        grid=(total // ROWS,),
        in_specs=[
            pl.BlockSpec((ROWS, width), lambda i: (i, 0)),
            pl.BlockSpec((width, both), lambda i: (0, 0), pipeline_mode=pl.Buffered(1)),
        ],
        out_specs=[
            pl.BlockSpec((ROWS, both), lambda i: (i, 0)),
            pl.BlockSpec((ROWS, both // 2), lambda i: (i, 0)),
        ],
        out_shape=[
            pltpu.HBM((total, both), jnp.float32),
            jax.ShapeDtypeStruct((total, both // 2), jnp.bfloat16),
        ],
        compiler_params=pltpu.CompilerParams(vmem_limit_bytes=24 << 20),
        name="forward_rows",
    )(rows, weights)


def backward_kernel(place_ref, d_ref, pre_ref, w_ref, grads_ref, back_ref):
    total = d_ref.shape[0]
    places = jnp.broadcast_to(place_ref[...], (ROWS, total))
    select = jnp.where(places == lax.broadcasted_iota(jnp.int32, (ROWS, total), 1), 1.0, 0.0)
    d_hidden = dot_plain(select.astype(jnp.bfloat16), d_ref[...])
    half = d_hidden.shape[1]
    gate_pre, up_pre = pre_ref[:, :half], pre_ref[:, half:]
    sigmoid_gate = jax.nn.sigmoid(gate_pre)
    d_gate = d_hidden * up_pre * sigmoid_gate * (1.0 + gate_pre * (1.0 - sigmoid_gate))
    d_up = d_hidden * gate_pre * sigmoid_gate
    grads_ref[:, :half] = d_gate.astype(jnp.bfloat16)
    grads_ref[:, half:] = d_up.astype(jnp.bfloat16)
    back_ref[...] = dot_plain(grads_ref[...], w_ref[...]).astype(jnp.bfloat16)


def backward(places, d_hidden, pre, weights):
    total, both = pre.shape
    width = weights.shape[1]
    return pl.pallas_call(
        backward_kernel,
        grid=(total // ROWS,),
        in_specs=[
            pl.BlockSpec((ROWS, 1), lambda i: (i, 0)),
            pl.BlockSpec((total, both // 2), lambda i: (0, 0), pipeline_mode=pl.Buffered(1)),
            pl.BlockSpec((ROWS, both), lambda i: (i, 0)),
            pl.BlockSpec((both, width), lambda i: (0, 0), pipeline_mode=pl.Buffered(1)),
        ],
        out_specs=[
            pl.BlockSpec((ROWS, both), lambda i: (i, 0)),
            pl.BlockSpec((ROWS, width), lambda i: (i, 0)),
        ],
        out_shape=[
            pltpu.HBM((total, both), jnp.bfloat16),
            pltpu.HBM((total, width), jnp.bfloat16),
        ],
        compiler_params=pltpu.CompilerParams(vmem_limit_bytes=24 << 20),
        name="backward_rows",
    )(places, d_hidden, pre, weights)


def outward_kernel(place_ref, hidden_ref, w_ref, hidden_out_ref, out_ref):
    total = hidden_ref.shape[0]
    places = jnp.broadcast_to(place_ref[...], (ROWS, total))
    select = jnp.where(places == lax.broadcasted_iota(jnp.int32, (ROWS, total), 1), 1.0, 0.0)
    hidden = dot_plain(select.astype(jnp.bfloat16), hidden_ref[...]).astype(jnp.bfloat16)
    hidden_out_ref[...] = hidden
    out_ref[...] = dot_plain(hidden, w_ref[...]).astype(jnp.bfloat16)


def outward(places, hidden, weights):
    total, part = hidden.shape
    width = weights.shape[1]
    return pl.pallas_call(
        outward_kernel,
        grid=(total // ROWS,),
        in_specs=[
            pl.BlockSpec((ROWS, 1), lambda i: (i, 0)),
            pl.BlockSpec((total, part), lambda i: (0, 0), pipeline_mode=pl.Buffered(1)),
            pl.BlockSpec((part, width), lambda i: (0, 0), pipeline_mode=pl.Buffered(1)),
        ],
        out_specs=[
            pl.BlockSpec((ROWS, part), lambda i: (i, 0)),
            pl.BlockSpec((ROWS, width), lambda i: (i, 0)),
        ],
        out_shape=[
            jax.ShapeDtypeStruct((total, part), jnp.bfloat16),
            pltpu.HBM((total, width), jnp.bfloat16),
        ],
        compiler_params=pltpu.CompilerParams(vmem_limit_bytes=24 << 20),
        name="outward_rows",
    )(places, hidden, weights)


PADDED = 8
INFO = 8


def spread_kernel(capacity, mine_ref, other_ref, out_ref):
    half, total = other_ref.shape[0], out_ref.shape[0]
    row, col = (lax.broadcasted_iota(jnp.int32, (total, half), axis) for axis in range(2))
    slot = lax.bitwise_and(row, PADDED - 1)
    source = lax.shift_right_logical(row, 4) * capacity + slot
    side = lax.bitwise_and(lax.shift_right_logical(row, 3), 1)
    found = (source == col) & (slot < capacity)
    parts = [
        dot_plain(jnp.where(found & (side == k), 1.0, 0.0).astype(jnp.bfloat16), rows)
        for k, rows in enumerate((mine_ref[:half, :], other_ref[...]))
    ]
    out_ref[...] = (parts[0] + parts[1]).astype(jnp.bfloat16)


def spread(mine, other, columns, capacity):
    return pl.pallas_call(
        functools.partial(spread_kernel, capacity),
        out_shape=jax.ShapeDtypeStruct((columns * 2 * PADDED, mine.shape[1]), jnp.bfloat16),
        compiler_params=pltpu.CompilerParams(vmem_limit_bytes=24 << 20),
        name="spread_rows",
    )(mine, other)


def prepare_kernel(tokens_ref, routes_ref, combine_ref, cot_ref, own_ref, send_ref, chosen_ref):
    count = tokens_ref.shape[0]
    square = (count, count)
    row, col = lax.broadcasted_iota(jnp.int32, square, 0), lax.broadcasted_iota(jnp.int32, square, 1)
    chosen = routes_ref[...].astype(jnp.float32)
    across = [jnp.broadcast_to(chosen[k : k + 1], square) for k in range(2)]
    down = [expert.T for expert in across]
    slots = [
        jnp.sum(
            jnp.where((row < col) & ((down[0] == expert) | (down[1] == expert)), 1.0, 0.0),
            axis=0,
            keepdims=True,
        )
        for expert in across
    ]
    own_ref[:count, :] = tokens_ref[...]
    own_ref[count:, :] = jnp.zeros((own_ref.shape[0] - count, own_ref.shape[1]), jnp.bfloat16)
    lines = [across[0][:1], across[1][:1], slots[0], slots[1], jnp.zeros((INFO - 4, count), jnp.float32)]
    own_ref[count:, :count] = jnp.concatenate(lines, axis=0).astype(jnp.bfloat16)
    cot = cot_ref[...].astype(jnp.float32)
    total = None
    for k in range(2):
        expert, slot = across[k][:1].astype(jnp.int32), slots[k].astype(jnp.int32)
        chosen_ref[k : k + 1, :] = expert
        chosen_ref[k + 2 : k + 3, :] = slot
        quarter, last = lax.shift_right_logical(expert, 2), lax.bitwise_and(expert, 1)
        pair = lax.bitwise_and(lax.shift_right_logical(expert, 1), 1)
        places = ((quarter * 2 + last) * 2 + pair) * PADDED + slot
        places = jnp.broadcast_to(places, (send_ref.shape[0], count))
        pick = jnp.where(lax.broadcasted_iota(jnp.int32, places.shape, 0) == places, 1.0, 0.0)
        weight = jnp.broadcast_to(combine_ref[k : k + 1], square).T[:, :1]
        weighted = (weight * cot).astype(jnp.bfloat16)
        part = dot_plain(pick.astype(jnp.bfloat16), weighted)
        total = part if total is None else total + part
    send_ref[...] = total.astype(jnp.bfloat16)


def prepare(tokens, routes, combine, cotangent, experts):
    count, width = tokens.shape
    return pl.pallas_call(
        prepare_kernel,
        out_shape=[
            jax.ShapeDtypeStruct((count + INFO, width), jnp.bfloat16),
            jax.ShapeDtypeStruct((experts * PADDED, width), jnp.bfloat16),
            jax.ShapeDtypeStruct((4, count), jnp.int32),
        ],
        compiler_params=pltpu.CompilerParams(vmem_limit_bytes=24 << 20),
        name="prepare_rows",
    )(*(pltpu.with_memory_space_constraint(x, pltpu.HBM) for x in (tokens, routes, combine, cotangent)))


def column_of(expert):
    return expert // 4 * 2 + expert % 2


def pair_of(expert):
    return expert // 2 % 2


def ring_shift(x, step):
    groups, experts = lax.axis_size("dp"), lax.axis_size("expert")
    pairs = []
    for group in range(groups):
        for expert in range(experts):
            z = (group * 2 + pair_of(expert) + step) % (2 * groups)
            target = z // 2 * experts + expert // 4 * 4 + z % 2 * 2 + expert % 2
            pairs.append((group * experts + expert, target))
    return lax.ppermute(x, ("dp", "expert"), pairs)


def group_shift(x, step):
    groups = lax.axis_size("dp")
    return lax.ppermute(x, "dp", [(g, (g + step) % groups) for g in range(groups)])


def pair_swap(x):
    experts = lax.axis_size("expert")
    return lax.ppermute(x, "expert", [(e, e + 2 - pair_of(e) * 4) for e in range(experts)])


def sum_of(*parts):
    total = parts[0].astype(jnp.float32)
    for part in parts[1:]:
        total = total + part.astype(jnp.float32)
    return total.astype(jnp.bfloat16)


def join(size, blocks):
    whole = jnp.zeros((size, blocks[0][1].shape[1]), blocks[0][1].dtype)
    for start, block in blocks:
        whole = lax.dynamic_update_slice_in_dim(whole, block, start, 0)
    return whole


def on_device(tokens, routes, combine, w_gate, w_up, w_down, cotangent):
    experts = lax.axis_size("expert")
    groups = lax.axis_size("dp")
    count = tokens.shape[0]
    width = tokens.shape[1]
    capacity = 10 * count // (4 * experts)
    slot_total = experts * capacity
    row_total = groups * slot_total
    columns = experts // 2
    planes = 2 * groups
    column_groups = [[e for e in range(experts) if pair_of(e) == pair] for pair in range(2)]
    ring_groups = [
        [g * experts + column // 2 * 4 + pair * 2 + column % 2 for g in range(groups) for pair in range(2)]
        for column in range(columns)
    ]
    everyone = ("dp", "expert")
    group = lax.axis_index("dp")
    place = lax.axis_index("expert")
    z = group * 2 + pair_of(place)

    own, send_cot, chosen = prepare(tokens, routes.T, combine.T, cotangent, experts)
    pair = pair_of(place)
    got = lax.all_to_all(
        send_cot.reshape(columns, 2 * PADDED, width),
        "expert",
        split_axis=0,
        concat_axis=0,
        tiled=True,
        axis_index_groups=column_groups,
    )
    got = [got[:, k * PADDED : k * PADDED + capacity].reshape(slot_total // 2, width) for k in range(2)]
    kept, passed = jnp.where(pair == 0, got[0], got[1]), jnp.where(pair == 0, got[1], got[0])
    got_cot = jnp.concatenate([kept, pair_swap(passed)], axis=0)
    cot = cotangent.astype(jnp.float32)
    target_row = (column_of(chosen[:2]) * 2 + (pair_of(chosen[:2]) != pair)) * PADDED + chosen[2:]
    positions = jnp.arange(columns * 2 * PADDED, dtype=jnp.int32)[:, None]
    pick_first = (positions == target_row[0:1]).astype(jnp.bfloat16)
    pick_second = (positions == target_row[1:2]).astype(jnp.bfloat16)

    held_count = count + INFO
    ring = lax.all_gather(own, everyone, axis_index_groups=ring_groups, axis=0, tiled=True)

    half_rows = slot_total // 2
    cot_rows = lax.all_gather(got_cot, "dp", axis=0, tiled=True)

    held = ring.reshape(planes, held_count, width)[:, count : count + 4, :count].astype(jnp.int32)
    block = jnp.arange(planes, dtype=jnp.int32)[:, None, None]
    ring_expert, ring_slot = held[:, 0:2], held[:, 2:4]
    ring_row = column_of(ring_expert) * (planes * capacity) + block * capacity + ring_slot
    here = pair_of(ring_expert) == pair_of(place)
    ring_row = jnp.where(here, ring_row, -1)
    held_row = jnp.pad(ring_row, ((0, 0), (0, 0), (0, held_count - count)), constant_values=-1)
    held_row = held_row.transpose(1, 0, 2).reshape(2, planes * held_count)
    send_tokens = select_rows(held_row, ring, row_total)
    token_rows = lax.all_to_all(
        send_tokens.reshape(columns, planes * capacity, width),
        "expert",
        split_axis=0,
        concat_axis=0,
        tiled=True,
        axis_index_groups=column_groups,
    ).reshape(row_total, width)

    ids = jnp.arange(row_total, dtype=jnp.int32)
    column, plane, slot = ids // (planes * capacity), ids // capacity % planes, ids % capacity
    cot_place = (plane // 2 * 2 + (plane % 2 != pair)) * (slot_total // 2) + column * capacity + slot
    side = ids // half_rows % 2
    out_plane = ids // slot_total * 2 + jnp.where(side == 1, 1 - pair, pair)
    out_place = (ids % half_rows // capacity * planes + out_plane) * capacity + ids % capacity

    down_w = w_down[0]
    up_gate_w = jnp.concatenate([w_gate[0], w_up[0]], axis=1)
    up_gate_wt = jnp.concatenate([w_gate[0].T, w_up[0].T], axis=0)
    pre, hidden = forward(token_rows, up_gate_w)
    hidden_cot, part_out = outward(out_place[:, None], hidden, down_w)
    expert_out = lax.psum_scatter(part_out, "dp", scatter_dimension=0, tiled=True)

    d_hidden = dot_last(cot_rows, down_w).astype(jnp.bfloat16)
    d_hidden, _ = lax.optimization_barrier((d_hidden, part_out))
    d_both, back_rows = backward(cot_place[:, None], d_hidden, pre, up_gate_wt)
    d_gate, d_up = d_both[:, : down_w.shape[0]], d_both[:, down_w.shape[0] :]
    arrived = lax.all_to_all(
        back_rows.reshape(columns, planes * capacity, width),
        "expert",
        split_axis=0,
        concat_axis=0,
        tiled=True,
        axis_index_groups=column_groups,
    ).reshape(row_total, width)
    token_row = ring_row.transpose(1, 0, 2).reshape(2, planes * count, 1)
    add_up = ((token_row[0] == ids[None, :]) | (token_row[1] == ids[None, :])).astype(jnp.bfloat16)
    d_ring = dot_plain(add_up, arrived).astype(jnp.bfloat16)
    d_tokens = lax.psum_scatter(
        d_ring, everyone, axis_index_groups=ring_groups, scatter_dimension=0, tiled=True
    )

    returned = lax.all_to_all(
        spread(expert_out, pair_swap(expert_out[half_rows:]), columns, capacity).reshape(columns, 2 * PADDED, width),
        "expert",
        split_axis=0,
        concat_axis=0,
        tiled=True,
        axis_index_groups=column_groups,
    ).reshape(columns * 2 * PADDED, width)
    first_out = dot_first(pick_first, returned)
    second_out = dot_first(pick_second, returned)
    out = (combine[:, 0:1] * first_out + combine[:, 1:2] * second_out).astype(jnp.bfloat16)
    d_combine = jnp.stack(
        [jnp.sum(cot * first_out, axis=1), jnp.sum(cot * second_out, axis=1)], axis=1
    )

    grad_gate = dot_first(token_rows, d_gate).astype(jnp.bfloat16)
    grad_up = dot_first(token_rows, d_up).astype(jnp.bfloat16)
    grad_down = dot_first(hidden_cot, cot_rows).astype(jnp.bfloat16)
    return (out, d_tokens, d_combine, grad_gate[None], grad_up[None], grad_down[None])


def solution(mesh):
    placed = (
        P(("dp", "expert"), None),
        P(("dp", "expert"), None),
        P(("dp", "expert"), None),
        P("expert", None, "dp"),
        P("expert", None, "dp"),
        P("expert", "dp", None),
        P(("dp", "expert"), None),
    )
    return jax.shard_map(
        on_device,
        mesh=mesh,
        in_specs=placed,
        out_specs=(
            P(("dp", "expert"), None),
            P(("dp", "expert"), None),
            P(("dp", "expert"), None),
            P("expert", None, "dp"),
            P("expert", None, "dp"),
            P("expert", "dp", None),
        ),
        check_vma=False,
    )
```

```python
import functools
import jax
import jax.numpy as jnp
from jax import lax
from jax.experimental import pallas as pl
from jax.experimental.pallas import tpu as pltpu
from jax.sharding import PartitionSpec as P


def dot_plain(left, right):
    return jnp.dot(left, right, preferred_element_type=jnp.float32)


def dot_last(left, right):
    return lax.dot_general(
        left, right, (((1,), (1,)), ((), ())), preferred_element_type=jnp.float32
    )


def dot_first(left, right):
    return lax.dot_general(
        left, right, (((0,), (0,)), ((), ())), preferred_element_type=jnp.float32
    )


ROWS = 320


def select_kernel(code_ref, x_ref, out_ref):
    row = pl.program_id(0) * ROWS + lax.broadcasted_iota(jnp.int32, (ROWS, x_ref.shape[0]), 0)
    found = (row == code_ref[:1]) | (row == code_ref[1:])
    select = jnp.where(found, 1.0, 0.0).astype(jnp.bfloat16)
    out_ref[...] = dot_plain(select, x_ref[...]).astype(jnp.bfloat16)


def select_rows(codes, x, total):
    held, width = x.shape
    return pl.pallas_call(
        select_kernel,
        grid=(total // ROWS,),
        in_specs=[
            pl.BlockSpec((2, held), lambda i: (0, 0), pipeline_mode=pl.Buffered(1)),
            pl.BlockSpec((held, width), lambda i: (0, 0), pipeline_mode=pl.Buffered(1)),
        ],
        out_specs=pl.BlockSpec((ROWS, width), lambda i: (i, 0)),
        out_shape=pltpu.HBM((total, width), jnp.bfloat16),
        compiler_params=pltpu.CompilerParams(vmem_limit_bytes=24 << 20),
        name="select_rows",
    )(codes, x)


def forward_kernel(x_ref, w_ref, pre_ref, hidden_ref):
    pre = dot_plain(x_ref[...], w_ref[...])
    pre_ref[...] = pre
    half = pre.shape[1] // 2
    gate_pre, up_pre = pre[:, :half], pre[:, half:]
    hidden_ref[...] = (gate_pre * jax.nn.sigmoid(gate_pre) * up_pre).astype(jnp.bfloat16)


def forward(rows, weights):
    total, width = rows.shape
    both = weights.shape[1]
    return pl.pallas_call(
        forward_kernel,
        grid=(total // ROWS,),
        in_specs=[
            pl.BlockSpec((ROWS, width), lambda i: (i, 0)),
            pl.BlockSpec((width, both), lambda i: (0, 0), pipeline_mode=pl.Buffered(1)),
        ],
        out_specs=[
            pl.BlockSpec((ROWS, both), lambda i: (i, 0)),
            pl.BlockSpec((ROWS, both // 2), lambda i: (i, 0)),
        ],
        out_shape=[
            pltpu.HBM((total, both), jnp.float32),
            jax.ShapeDtypeStruct((total, both // 2), jnp.bfloat16),
        ],
        compiler_params=pltpu.CompilerParams(vmem_limit_bytes=24 << 20),
        name="forward_rows",
    )(rows, weights)


def backward_kernel(place_ref, d_ref, pre_ref, w_ref, grads_ref, back_ref):
    total = d_ref.shape[0]
    places = jnp.broadcast_to(place_ref[...], (ROWS, total))
    select = jnp.where(places == lax.broadcasted_iota(jnp.int32, (ROWS, total), 1), 1.0, 0.0)
    d_hidden = dot_plain(select.astype(jnp.bfloat16), d_ref[...])
    half = d_hidden.shape[1]
    gate_pre, up_pre = pre_ref[:, :half], pre_ref[:, half:]
    sigmoid_gate = jax.nn.sigmoid(gate_pre)
    d_gate = d_hidden * up_pre * sigmoid_gate * (1.0 + gate_pre * (1.0 - sigmoid_gate))
    d_up = d_hidden * gate_pre * sigmoid_gate
    grads_ref[:, :half] = d_gate.astype(jnp.bfloat16)
    grads_ref[:, half:] = d_up.astype(jnp.bfloat16)
    back_ref[...] = dot_plain(grads_ref[...], w_ref[...]).astype(jnp.bfloat16)


def backward(places, d_hidden, pre, weights):
    total, both = pre.shape
    width = weights.shape[1]
    return pl.pallas_call(
        backward_kernel,
        grid=(total // ROWS,),
        in_specs=[
            pl.BlockSpec((ROWS, 1), lambda i: (i, 0)),
            pl.BlockSpec((total, both // 2), lambda i: (0, 0), pipeline_mode=pl.Buffered(1)),
            pl.BlockSpec((ROWS, both), lambda i: (i, 0)),
            pl.BlockSpec((both, width), lambda i: (0, 0), pipeline_mode=pl.Buffered(1)),
        ],
        out_specs=[
            pl.BlockSpec((ROWS, both), lambda i: (i, 0)),
            pl.BlockSpec((ROWS, width), lambda i: (i, 0)),
        ],
        out_shape=[
            pltpu.HBM((total, both), jnp.bfloat16),
            pltpu.HBM((total, width), jnp.bfloat16),
        ],
        compiler_params=pltpu.CompilerParams(vmem_limit_bytes=24 << 20),
        name="backward_rows",
    )(places, d_hidden, pre, weights)


def outward_kernel(place_ref, hidden_ref, w_ref, hidden_out_ref, out_ref):
    total = hidden_ref.shape[0]
    places = jnp.broadcast_to(place_ref[...], (ROWS, total))
    select = jnp.where(places == lax.broadcasted_iota(jnp.int32, (ROWS, total), 1), 1.0, 0.0)
    hidden = dot_plain(select.astype(jnp.bfloat16), hidden_ref[...]).astype(jnp.bfloat16)
    hidden_out_ref[...] = hidden
    out_ref[...] = dot_plain(hidden, w_ref[...]).astype(jnp.bfloat16)


def outward(places, hidden, weights):
    total, part = hidden.shape
    width = weights.shape[1]
    return pl.pallas_call(
        outward_kernel,
        grid=(total // ROWS,),
        in_specs=[
            pl.BlockSpec((ROWS, 1), lambda i: (i, 0)),
            pl.BlockSpec((total, part), lambda i: (0, 0), pipeline_mode=pl.Buffered(1)),
            pl.BlockSpec((part, width), lambda i: (0, 0), pipeline_mode=pl.Buffered(1)),
        ],
        out_specs=[
            pl.BlockSpec((ROWS, part), lambda i: (i, 0)),
            pl.BlockSpec((ROWS, width), lambda i: (i, 0)),
        ],
        out_shape=[
            jax.ShapeDtypeStruct((total, part), jnp.bfloat16),
            pltpu.HBM((total, width), jnp.bfloat16),
        ],
        compiler_params=pltpu.CompilerParams(vmem_limit_bytes=24 << 20),
        name="outward_rows",
    )(places, hidden, weights)


PADDED = 8
INFO = 8


def spread_kernel(capacity, mine_ref, other_ref, out_ref):
    half, total = other_ref.shape[0], out_ref.shape[0]
    row, col = (lax.broadcasted_iota(jnp.int32, (total, half), axis) for axis in range(2))
    slot = lax.bitwise_and(row, PADDED - 1)
    source = lax.shift_right_logical(row, 4) * capacity + slot
    side = lax.bitwise_and(lax.shift_right_logical(row, 3), 1)
    found = (source == col) & (slot < capacity)
    parts = [
        dot_plain(jnp.where(found & (side == k), 1.0, 0.0).astype(jnp.bfloat16), rows)
        for k, rows in enumerate((mine_ref[:half, :], other_ref[...]))
    ]
    out_ref[...] = (parts[0] + parts[1]).astype(jnp.bfloat16)


def spread(mine, other, columns, capacity):
    return pl.pallas_call(
        functools.partial(spread_kernel, capacity),
        out_shape=jax.ShapeDtypeStruct((columns * 2 * PADDED, mine.shape[1]), jnp.bfloat16),
        compiler_params=pltpu.CompilerParams(vmem_limit_bytes=24 << 20),
        name="spread_rows",
    )(mine, other)


def prepare_kernel(tokens_ref, routes_ref, combine_ref, cot_ref, own_ref, send_ref, chosen_ref):
    count = tokens_ref.shape[0]
    square = (count, count)
    row, col = lax.broadcasted_iota(jnp.int32, square, 0), lax.broadcasted_iota(jnp.int32, square, 1)
    chosen = routes_ref[...].astype(jnp.float32)
    across = [jnp.broadcast_to(chosen[k : k + 1], square) for k in range(2)]
    down = [expert.T for expert in across]
    slots = [
        jnp.sum(
            jnp.where((row < col) & ((down[0] == expert) | (down[1] == expert)), 1.0, 0.0),
            axis=0,
            keepdims=True,
        )
        for expert in across
    ]
    own_ref[:count, :] = tokens_ref[...]
    own_ref[count:, :] = jnp.zeros((own_ref.shape[0] - count, own_ref.shape[1]), jnp.bfloat16)
    lines = [across[0][:1], across[1][:1], slots[0], slots[1], jnp.zeros((INFO - 4, count), jnp.float32)]
    own_ref[count:, :count] = jnp.concatenate(lines, axis=0).astype(jnp.bfloat16)
    cot = cot_ref[...].astype(jnp.float32)
    total = None
    for k in range(2):
        expert, slot = across[k][:1].astype(jnp.int32), slots[k].astype(jnp.int32)
        chosen_ref[k : k + 1, :] = expert
        chosen_ref[k + 2 : k + 3, :] = slot
        quarter, last = lax.shift_right_logical(expert, 2), lax.bitwise_and(expert, 1)
        pair = lax.bitwise_and(lax.shift_right_logical(expert, 1), 1)
        places = ((quarter * 2 + last) * 2 + pair) * PADDED + slot
        places = jnp.broadcast_to(places, (send_ref.shape[0], count))
        pick = jnp.where(lax.broadcasted_iota(jnp.int32, places.shape, 0) == places, 1.0, 0.0)
        weight = jnp.broadcast_to(combine_ref[k : k + 1], square).T[:, :1]
        weighted = (weight * cot).astype(jnp.bfloat16)
        part = dot_plain(pick.astype(jnp.bfloat16), weighted)
        total = part if total is None else total + part
    send_ref[...] = total.astype(jnp.bfloat16)


def prepare(tokens, routes, combine, cotangent, experts):
    count, width = tokens.shape
    return pl.pallas_call(
        prepare_kernel,
        out_shape=[
            jax.ShapeDtypeStruct((count + INFO, width), jnp.bfloat16),
            jax.ShapeDtypeStruct((experts * PADDED, width), jnp.bfloat16),
            jax.ShapeDtypeStruct((4, count), jnp.int32),
        ],
        compiler_params=pltpu.CompilerParams(vmem_limit_bytes=24 << 20),
        name="prepare_rows",
    )(*(pltpu.with_memory_space_constraint(x, pltpu.HBM) for x in (tokens, routes, combine, cotangent)))


def column_of(expert):
    return expert // 4 * 2 + expert % 2


def pair_of(expert):
    return expert // 2 % 2


def ring_shift(x, step):
    groups, experts = lax.axis_size("dp"), lax.axis_size("expert")
    pairs = []
    for group in range(groups):
        for expert in range(experts):
            z = (group * 2 + pair_of(expert) + step) % (2 * groups)
            target = z // 2 * experts + expert // 4 * 4 + z % 2 * 2 + expert % 2
            pairs.append((group * experts + expert, target))
    return lax.ppermute(x, ("dp", "expert"), pairs)


def group_shift(x, step):
    groups = lax.axis_size("dp")
    return lax.ppermute(x, "dp", [(g, (g + step) % groups) for g in range(groups)])


def pair_swap(x):
    experts = lax.axis_size("expert")
    return lax.ppermute(x, "expert", [(e, e + 2 - pair_of(e) * 4) for e in range(experts)])


def sum_of(*parts):
    total = parts[0].astype(jnp.float32)
    for part in parts[1:]:
        total = total + part.astype(jnp.float32)
    return total.astype(jnp.bfloat16)


def join(size, blocks):
    whole = jnp.zeros((size, blocks[0][1].shape[1]), blocks[0][1].dtype)
    for start, block in blocks:
        whole = lax.dynamic_update_slice_in_dim(whole, block, start, 0)
    return whole


def on_device(tokens, routes, combine, w_gate, w_up, w_down, cotangent):
    experts = lax.axis_size("expert")
    groups = lax.axis_size("dp")
    count = tokens.shape[0]
    width = tokens.shape[1]
    capacity = 10 * count // (4 * experts)
    slot_total = experts * capacity
    row_total = groups * slot_total
    columns = experts // 2
    planes = 2 * groups
    column_groups = [[e for e in range(experts) if pair_of(e) == pair] for pair in range(2)]
    ring_groups = [
        [g * experts + column // 2 * 4 + pair * 2 + column % 2 for g in range(groups) for pair in range(2)]
        for column in range(columns)
    ]
    everyone = ("dp", "expert")
    group = lax.axis_index("dp")
    place = lax.axis_index("expert")
    z = group * 2 + pair_of(place)

    own, send_cot, chosen = prepare(tokens, routes.T, combine.T, cotangent, experts)
    pair = pair_of(place)
    got = lax.all_to_all(
        send_cot.reshape(columns, 2 * PADDED, width),
        "expert",
        split_axis=0,
        concat_axis=0,
        tiled=True,
        axis_index_groups=column_groups,
    )
    got = [got[:, k * PADDED : k * PADDED + capacity].reshape(slot_total // 2, width) for k in range(2)]
    kept, passed = jnp.where(pair == 0, got[0], got[1]), jnp.where(pair == 0, got[1], got[0])
    got_cot = jnp.concatenate([kept, pair_swap(passed)], axis=0)
    cot = cotangent.astype(jnp.float32)
    target_row = (column_of(chosen[:2]) * 2 + (pair_of(chosen[:2]) != pair)) * PADDED + chosen[2:]
    positions = jnp.arange(columns * 2 * PADDED, dtype=jnp.int32)[:, None]
    pick_first = (positions == target_row[0:1]).astype(jnp.bfloat16)
    pick_second = (positions == target_row[1:2]).astype(jnp.bfloat16)

    held_count = count + INFO
    ring = lax.all_gather(own, everyone, axis_index_groups=ring_groups, axis=0, tiled=True)

    half_rows = slot_total // 2
    cot_rows = lax.all_gather(got_cot, "dp", axis=0, tiled=True)

    held = ring.reshape(planes, held_count, width)[:, count : count + 4, :count].astype(jnp.int32)
    block = jnp.arange(planes, dtype=jnp.int32)[:, None, None]
    ring_expert, ring_slot = held[:, 0:2], held[:, 2:4]
    ring_row = column_of(ring_expert) * (planes * capacity) + block * capacity + ring_slot
    here = pair_of(ring_expert) == pair_of(place)
    ring_row = jnp.where(here, ring_row, -1)
    held_row = jnp.pad(ring_row, ((0, 0), (0, 0), (0, held_count - count)), constant_values=-1)
    held_row = held_row.transpose(1, 0, 2).reshape(2, planes * held_count)
    send_tokens = select_rows(held_row, ring, row_total)
    token_rows = lax.all_to_all(
        send_tokens.reshape(columns, planes * capacity, width),
        "expert",
        split_axis=0,
        concat_axis=0,
        tiled=True,
        axis_index_groups=column_groups,
    ).reshape(row_total, width)

    ids = jnp.arange(row_total, dtype=jnp.int32)
    column, plane, slot = ids // (planes * capacity), ids // capacity % planes, ids % capacity
    cot_place = (plane // 2 * 2 + (plane % 2 != pair)) * (slot_total // 2) + column * capacity + slot
    side = ids // half_rows % 2
    out_plane = ids // slot_total * 2 + jnp.where(side == 1, 1 - pair, pair)
    out_place = (ids % half_rows // capacity * planes + out_plane) * capacity + ids % capacity

    down_w = w_down[0]
    up_gate_w = jnp.concatenate([w_gate[0], w_up[0]], axis=1)
    up_gate_wt = jnp.concatenate([w_gate[0].T, w_up[0].T], axis=0)
    pre, hidden = forward(token_rows, up_gate_w)
    hidden_cot, part_out = outward(out_place[:, None], hidden, down_w)
    expert_out = lax.psum_scatter(part_out, "dp", scatter_dimension=0, tiled=True)

    d_hidden = dot_last(cot_rows, down_w).astype(jnp.bfloat16)
    d_hidden, _ = lax.optimization_barrier((d_hidden, part_out))
    d_both, back_rows = backward(cot_place[:, None], d_hidden, pre, up_gate_wt)
    d_gate, d_up = d_both[:, : down_w.shape[0]], d_both[:, down_w.shape[0] :]
    arrived = lax.all_to_all(
        back_rows.reshape(columns, planes * capacity, width),
        "expert",
        split_axis=0,
        concat_axis=0,
        tiled=True,
        axis_index_groups=column_groups,
    ).reshape(row_total, width)
    token_row = ring_row.transpose(1, 0, 2).reshape(2, planes * count, 1)
    add_up = ((token_row[0] == ids[None, :]) | (token_row[1] == ids[None, :])).astype(jnp.bfloat16)
    d_ring = dot_plain(add_up, arrived).astype(jnp.bfloat16)
    d_tokens = lax.psum_scatter(
        d_ring, everyone, axis_index_groups=ring_groups, scatter_dimension=0, tiled=True
    )

    returned = lax.all_to_all(
        spread(expert_out, pair_swap(expert_out[half_rows:]), columns, capacity).reshape(columns, 2 * PADDED, width),
        "expert",
        split_axis=0,
        concat_axis=0,
        tiled=True,
        axis_index_groups=column_groups,
    ).reshape(columns * 2 * PADDED, width)
    first_out = dot_first(pick_first, returned)
    second_out = dot_first(pick_second, returned)
    out = (combine[:, 0:1] * first_out + combine[:, 1:2] * second_out).astype(jnp.bfloat16)
    d_combine = jnp.stack(
        [jnp.sum(cot * first_out, axis=1), jnp.sum(cot * second_out, axis=1)], axis=1
    )

    grad_gate = dot_first(token_rows, d_gate).astype(jnp.bfloat16)
    grad_up = dot_first(token_rows, d_up).astype(jnp.bfloat16)
    grad_down = dot_first(hidden_cot, cot_rows).astype(jnp.bfloat16)
    return (out, d_tokens, d_combine, grad_gate[None], grad_up[None], grad_down[None])


def solution(mesh):
    placed = (
        P(("dp", "expert"), None),
        P(("dp", "expert"), None),
        P(("dp", "expert"), None),
        P("expert", None, "dp"),
        P("expert", None, "dp"),
        P("expert", "dp", None),
        P(("dp", "expert"), None),
    )
    return jax.shard_map(
        on_device,
        mesh=mesh,
        in_specs=placed,
        out_specs=(
            P(("dp", "expert"), None),
            P(("dp", "expert"), None),
            P(("dp", "expert"), None),
            P("expert", None, "dp"),
            P("expert", None, "dp"),
            P("expert", "dp", None),
        ),
        check_vma=False,
    )
```
